128 devices in a mesh: head: 8 (over z, core), ctx: 16 (over x, y).
Axes of the slice: x: 4, y: 4, z: 4, core: 2. Of those that a mesh axis runs over, the one named last changes fastest.
Arguments:
- queries: bfloat16 [16384, 8, 128], P('ctx', 'head'), may hold values from -120 to 120
- keys: bfloat16 [16384, 8, 128], P('ctx', 'head'), may hold values from -6 to 6
- values: bfloat16 [16384, 8, 128], P('ctx', 'head'), may hold values from -6 to 6
- house: bfloat16 [16384, 8, 128], P('ctx', 'head'), may hold values from -6 to 6
- rates: float32 [8, 16384], P('head', 'ctx'), may hold values from 0.0002 to 1.9, as said below
- out_weight: bfloat16 [1024, 8192], P('head'), may hold values from -0.25 to 0.25
Outputs:
- attended: bfloat16 [16384, 8, 128], P('ctx', 'head')
- projected: bfloat16 [16384, 8192], P('ctx', 'head')
The draws below stay inside these ranges and needn't reach their ends.
Inputs may be any that keep to these rules, and one draw needn't show every extreme that they name: `rates`: strictly positive and below 2, so every transition is a contraction.
All inputs are finite; a program needn't handle non-finite values.
Results may differ from the reference program's by a relative error of at most 0.015.
Values may be sent and summed in bfloat16 or wider, within the bound.
No kernel may reach another device: no remote copies, remote signals or barrier semaphores. Data moves between devices by JAX's collectives and lax.ppermute only.
A program may use at most 64 MiB of HBM per device.

```python
import jax
import jax.numpy as jnp
from jax import lax

DH = 128
DMODEL = 8192
BLOCK = 128
TOK_DEV = 1024
SHARD_ATTN_COUNT = 8
PROMPT_LENGTH = 16384
N_CTX = 16


def key_base(key):
    return jnp.clip(jax.random.normal(jax.random.fold_in(key, 31), (PROMPT_LENGTH, SHARD_ATTN_COUNT, DH), jnp.float32), -6.0, 6.0)


def draw_keys(key, part):
    return key_base(key).astype(jnp.bfloat16)


def draw_queries(key, part):
    drawn = jnp.clip(2.0 * jax.random.normal(jax.random.fold_in(key, 47), (PROMPT_LENGTH, SHARD_ATTN_COUNT, DH), jnp.float32), -12.0, 12.0)
    return drawn.astype(jnp.bfloat16)


def draw_rates(key, part):
    head_key = jax.random.fold_in(key, 61)
    jitter_key = jax.random.fold_in(key, 67)
    spike_draw_seed = jax.random.fold_in(key, 71)
    spot_key = jax.random.fold_in(key, 73)
    lowest, highest = (0.002, 0.6)
    head_rate = jnp.exp(jax.random.uniform(head_key, (SHARD_ATTN_COUNT, 1), jnp.float32, jnp.log(lowest), jnp.log(highest)))
    random_noise = jnp.exp(jax.random.uniform(jitter_key, (SHARD_ATTN_COUNT, PROMPT_LENGTH), jnp.float32, jnp.log(0.5), jnp.log(2.0)))
    spots = jax.random.randint(spot_key, (6,), 0, PROMPT_LENGTH)
    position = jnp.arange(PROMPT_LENGTH)
    struck = jnp.any(position[:, None] == spots[None, :], axis=1)
    steep_forgetting = jax.random.uniform(spike_draw_seed, (SHARD_ATTN_COUNT, PROMPT_LENGTH), jnp.float32, 0.8, 1.5)
    steady = jnp.clip(head_rate * random_noise, 0.0002, 1.9)
    return jnp.where(struck[None, :], steep_forgetting, steady).astype(jnp.float32)


def spiked(values, key, source, target, parts, factor):
    owner, partner = [(jnp.arange(values.shape[dim]) // (values.shape[dim] // parts)).reshape([-1 if axis == dim else 1 for axis in range(values.ndim)]) for dim in (source, target)]
    chosen = jax.random.permutation(key, parts)[partner]
    strong = (owner == chosen) | (owner == (partner + parts // 2) % parts)
    return jnp.where(strong, factor * values, values)


def block_scale(key, shape, split, least, largest):
    def one(dim, parts):
        steps = jax.random.uniform(jax.random.fold_in(jax.random.fold_in(key, 6), dim), (parts,), jnp.float32, least / len(split), largest / len(split))
        return jnp.repeat(jnp.exp(steps), shape[dim] // parts).reshape((-1,) + (1,) * (len(shape) - dim - 1))

    loudness = one(*split[0])
    for cut in split[1:]:
        loudness = loudness * one(*cut)
    return loudness


def centred(rng, shape, deviation, bound, pieces=(), kind=jnp.bfloat16):
    loudness = block_scale(rng, shape, pieces, -0.22, 0.18) if pieces else 1.0
    drawn = jax.random.normal(rng, shape, jnp.float32) * deviation * loudness
    return jnp.minimum(jnp.maximum(drawn, -bound), bound).astype(kind)


def heavy_noise(key, shape, spread, bound, shards, heavy, held_as=jnp.bfloat16):
    values = spread * jax.random.normal(key, shape, jnp.float32)
    if shards:
        values = values * block_scale(key, shape, shards, -0.22, 0.18)
    return jnp.clip(spiked(values, jax.random.fold_in(key, 3), *heavy), -bound, bound).astype(held_as)


def setup_inputs(seed: int = 0) -> dict:
    streams_of = jax.random.split(jax.random.key(seed), 7)
    return {
        "queries": draw_queries(jax.random.fold_in(streams_of[6], 71), 0),
        "keys": draw_keys(jax.random.fold_in(streams_of[6], 71), 0),
        "values": centred(streams_of[2], (PROMPT_LENGTH, SHARD_ATTN_COUNT, DH), 1.0, 6.0, ((0, 16), (1, 8))),
        "house": centred(streams_of[3], (PROMPT_LENGTH, SHARD_ATTN_COUNT, DH), 1.0, 6.0, ((0, 16), (1, 8))),
        "rates": draw_rates(jax.random.fold_in(streams_of[6], 71), 0),
        "out_weight": heavy_noise(streams_of[5], (SHARD_ATTN_COUNT * DH, DMODEL), (SHARD_ATTN_COUNT * DH) ** -0.5, 0.25, ((0, 8),), (0, 1, 8, 2.0)),
    }


EPSILON = 1e-06
NEGATIVE = -1e+30
PRECISE = lax.Precision.HIGHEST

def matmul(first_matrix, second_matrix):
    return jnp.matmul(first_matrix, second_matrix, precision=PRECISE)

def block_parts(query_rows, key_rows, house_rows, decays):
    length = query_rows.shape[0]
    features = query_rows.shape[1]
    row_index = lax.broadcasted_iota(jnp.int32, (length, length), 0)
    col_index = lax.broadcasted_iota(jnp.int32, (length, length), 1)
    gram_matrix = matmul(house_rows, house_rows.T)
    zero_block = jnp.zeros_like(gram_matrix)
    lower_part = jnp.where(row_index > col_index, gram_matrix, zero_block) + jnp.diag(1.0 / decays)
    identity = jnp.eye(length, dtype=query_rows.dtype)
    inverse = jax.scipy.linalg.solve_triangular(lower_part, identity, lower=True)
    left_part = jnp.where(row_index >= col_index, matmul(query_rows, house_rows.T), zero_block)
    right_part = matmul(inverse, jnp.where(row_index > col_index, matmul(house_rows, key_rows.T), zero_block))
    start_query = query_rows - matmul(matmul(left_part, inverse), house_rows)
    final_key = key_rows - matmul(right_part.T, house_rows)
    inside_mask = matmul(query_rows, key_rows.T) - matmul(left_part, right_part)
    inside_mask = jnp.where(row_index >= col_index, inside_mask, NEGATIVE)
    passage = jnp.eye(features, dtype=query_rows.dtype) - matmul(house_rows.T, matmul(inverse, house_rows))
    return (start_query, final_key, inside_mask, passage)

def shard_local(start_query, final_key, inside_mask, passage):
    blocks, length, features = start_query.shape
    rows_dev = blocks * length
    col_block = lax.broadcasted_iota(jnp.int32, (length, rows_dev), 1) // length
    anchor = jnp.zeros((), jnp.int32)

    def advance(running, element):
        moved_keys, prefix = running
        number, query_rows, key_rows, inside_rows, passage_rows = element
        across = matmul(query_rows, moved_keys.T)
        scores = jnp.where(col_block < number, across, NEGATIVE)
        scores = lax.dynamic_update_slice(scores, inside_rows, (anchor, number * length))
        carried_query = matmul(query_rows, prefix)
        moved_keys = matmul(moved_keys, passage_rows.T)
        moved_keys = lax.dynamic_update_slice(moved_keys, key_rows, (number * length, anchor))
        prefix = matmul(passage_rows, prefix)
        return ((moved_keys, prefix), (scores, carried_query))
    numbers = jnp.arange(blocks, dtype=jnp.int32)
    initial = (jnp.zeros((rows_dev, features), start_query.dtype), jnp.eye(features, dtype=start_query.dtype))
    (end_keys, transit), (scores, carried) = lax.scan(advance, initial, (numbers, start_query, final_key, inside_mask, passage))
    return (scores.reshape(rows_dev, rows_dev), carried.reshape(rows_dev, features), end_keys, transit)

def head_attention(query_all, key_all, value_all, house_all, decays):
    features = query_all.shape[1]
    blocks = PROMPT_LENGTH // BLOCK
    query_f = query_all.astype(jnp.float32) * features ** (-0.5)
    key_f = key_all.astype(jnp.float32)
    house_f = house_all.astype(jnp.float32)
    house_unit = house_f / jnp.sqrt(lax.optimization_barrier(jnp.sum(house_f * house_f, axis=1, keepdims=True)) + EPSILON)
    block_data = jax.vmap(block_parts)(query_f.reshape(blocks, BLOCK, features), key_f.reshape(blocks, BLOCK, features), house_unit.reshape(blocks, BLOCK, features), decays.reshape(blocks, BLOCK))
    per_shard = [array.reshape((N_CTX, TOK_DEV // BLOCK) + array.shape[1:]) for array in block_data]
    scores_local, carried, end_keys, transit = jax.vmap(shard_local)(*per_shard)
    stored_keys = end_keys.astype(jnp.bfloat16).astype(jnp.float32)
    value_blocks = value_all.astype(jnp.float32).reshape(N_CTX, TOK_DEV, features)
    anchor = jnp.zeros((), jnp.int32)

    def shard_rows(number):
        start_rows = lax.dynamic_index_in_dim(carried, number, 0, keepdims=False)
        own_scores = lax.dynamic_index_in_dim(scores_local, number, 0, keepdims=False)
        row_scores = jnp.full((TOK_DEV, PROMPT_LENGTH), NEGATIVE, query_f.dtype)
        row_scores = lax.dynamic_update_slice(row_scores, own_scores, (anchor, number * TOK_DEV))

        def visit_shard(offset, running):
            moving, table_scores = running
            source = number - 1 - offset
            block_keys = lax.dynamic_index_in_dim(stored_keys, source, 0, keepdims=False)
            table_scores = lax.dynamic_update_slice(table_scores, matmul(moving, block_keys.T), (anchor, source * TOK_DEV))
            moving = matmul(moving, lax.dynamic_index_in_dim(transit, source, 0, keepdims=False))
            return (moving, table_scores)
        _, row_scores = lax.fori_loop(anchor, number, visit_shard, (start_rows, row_scores))
        row_peak = lax.optimization_barrier(jnp.max(row_scores, axis=1, keepdims=True))
        weight_matrix = jnp.exp(row_scores - row_peak)
        totals = lax.optimization_barrier(jnp.sum(weight_matrix, axis=1))
        rounded = lax.optimization_barrier(weight_matrix.astype(jnp.bfloat16)).astype(jnp.float32)

        def gather_values(source, summed):
            weight_piece = lax.dynamic_slice_in_dim(rounded, source * TOK_DEV, TOK_DEV, 1)
            value_piece = lax.dynamic_index_in_dim(value_blocks, source, 0, keepdims=False)
            return summed + matmul(weight_piece, value_piece)
        summed = lax.fori_loop(anchor, number + 1, gather_values, jnp.zeros((TOK_DEV, features), query_f.dtype))
        return (summed / totals[:, None]).astype(jnp.bfloat16)
    outputs = lax.map(shard_rows, jnp.arange(N_CTX, dtype=jnp.int32))
    return outputs.reshape(PROMPT_LENGTH, features)

def reference(queries, keys, values, house, rates, out_weight):

    def select_head(number):
        return head_attention(lax.dynamic_index_in_dim(queries, number, 1, keepdims=False), lax.dynamic_index_in_dim(keys, number, 1, keepdims=False), lax.dynamic_index_in_dim(values, number, 1, keepdims=False), lax.dynamic_index_in_dim(house, number, 1, keepdims=False), lax.dynamic_index_in_dim(rates, number, 0, keepdims=False))
    per_head = lax.map(select_head, jnp.arange(SHARD_ATTN_COUNT, dtype=jnp.int32))
    attended = jnp.transpose(per_head, (1, 0, 2))
    flattened = attended.reshape(PROMPT_LENGTH, SHARD_ATTN_COUNT * DH)
    projected = matmul(flattened.astype(jnp.float32), out_weight.astype(jnp.float32))
    return (attended, projected.astype(jnp.bfloat16))
```

```python
import jax
import jax.numpy as jnp
from jax import lax
from jax.experimental import pallas as pl
from jax.experimental.pallas import tpu as pltpu
from jax.sharding import PartitionSpec as P

C = 128
F32 = jnp.float32
BF16 = jnp.bfloat16
EPSILON = 1e-06
NEGATIVE = -1e30
LOG2E = 1.4426950408889634
VMEM_LIMIT = 56 * 1024 * 1024


def split(x):
    high = x.astype(BF16)
    return high, (x - high.astype(F32)).astype(BF16)


def left(x):
    return jnp.concatenate(split(x), axis=1)


def right_nn(x):
    pair = jnp.concatenate(split(x), axis=1)
    return jnp.concatenate([pair, pair], axis=0)


def right_nt(x):
    high, low = split(x)
    return jnp.concatenate(
        [jnp.concatenate([high, high], axis=1), jnp.concatenate([low, low], axis=1)], axis=0
    )


def halves(x):
    return x[:, : x.shape[1] // 2] + x[:, x.shape[1] // 2 :]


def nn(a, b):
    return halves(jnp.dot(a, b, preferred_element_type=F32))


def contract_last(a, b):
    return lax.dot_general(a, b, (((1,), (1,)), ((), ())), preferred_element_type=F32)


def nt(a, b):
    return halves(contract_last(a, b))


def unit_house(house):
    raw = house.astype(F32)
    return raw / jnp.sqrt(jnp.sum(raw * raw, axis=1, keepdims=True) + EPSILON)


def transport_kernel(keys, house, rates, sent, passages, inverses, rights, finals, unit):
    blocks = rates.shape[0]
    row = lax.broadcasted_iota(jnp.int32, (C, C), 0)
    col = lax.broadcasted_iota(jnp.int32, (C, C), 1)
    eye = jnp.where(row == col, 1.0, 0.0).astype(F32)
    every = range(blocks)
    w = [unit_house(house[pl.ds(n * C, C), :]) for n in every]
    for n in every:
        unit[pl.ds(n * C, C), :] = w[n]
    wl = [left(x) for x in w]
    strict = []
    for n in every:
        gram = nt(wl[n], right_nt(w[n]))
        decay = jnp.transpose(jnp.broadcast_to(rates[n : n + 1, :], (C, C)))
        strict.append(jnp.where(row > col, gram, 0.0) * decay)
    x = [eye - jnp.where((row // 2) == (col // 2), strict[n], 0.0) for n in every]
    size = 2
    while size < C:
        band = ((row // (2 * size)) == (col // (2 * size))) & ((row // size) != (col // size))
        inner = [nn(left(jnp.where(band, strict[n], 0.0)), right_nn(x[n])) for n in every]
        x = [x[n] - nn(left(x[n]), right_nn(inner[n])) for n in every]
        size *= 2
    t = [x[n] * rates[n : n + 1, :] for n in every]
    for n in every:
        inverses[n] = t[n]
    final = []
    for n in every:
        k = keys[pl.ds(n * C, C), :]
        met = jnp.where(col > row, contract_last(jnp.concatenate([k, k], axis=1), wl[n]), 0.0)
        r = nt(left(met), right_nt(t[n]))
        rights[n] = r
        f = k.astype(F32) - nn(left(r), right_nn(w[n]))
        finals[pl.ds(n * C, C), :] = f
        final.append(f)
    passage = []
    for n in every:
        u = nn(left(t[n]), right_nn(w[n]))
        passage.append(eye - nn(left(jnp.transpose(w[n])), right_nn(u)))
        passages[n] = passage[n]
    sent[pl.ds((blocks - 1) * C, C), :] = final[blocks - 1].astype(BF16)
    s = passage[blocks - 1]
    for n in range(blocks - 2, -1, -1):
        sent[pl.ds(n * C, C), :] = nt(left(final[n]), right_nt(s)).astype(BF16)
        s = nn(left(s), right_nn(passage[n]))
    high, low = split(s)
    sent[pl.ds(blocks * C, C), :] = high
    sent[pl.ds((blocks + 1) * C, C), :] = low


def transport(keys, house, rates):
    rows = keys.shape[0]
    blocks = rows // C
    square = jax.ShapeDtypeStruct((blocks, C, C), F32)
    flat = jax.ShapeDtypeStruct((rows, C), F32)
    return pl.pallas_call(
        transport_kernel,
        out_shape=(jax.ShapeDtypeStruct((rows + 2 * C, C), BF16), square, square, square, flat, flat),
        compiler_params=pltpu.CompilerParams(vmem_limit_bytes=VMEM_LIMIT),
        name="transport",
    )(keys, house, rates)


def own_kernel(
    queries, keys, values, passages, inverses, rights, finals, unit, moved, peak, total, summed, table, moving
):
    blocks = passages.shape[0]
    row = lax.broadcasted_iota(jnp.int32, (C, C), 0)
    col = lax.broadcasted_iota(jnp.int32, (C, C), 1)
    for n in range(blocks):
        here = pl.ds(n * C, C)
        q = queries[here, :].astype(F32) * (C**-0.5 * LOG2E)
        w = unit[here, :]
        k = keys[here, :]
        ql = left(q)
        seen = left(jnp.where(row >= col, nt(ql, right_nt(w)), 0.0))
        start = q - nn(left(nn(seen, right_nn(inverses[n]))), right_nn(w))
        inside = contract_last(ql, jnp.concatenate([k, k], axis=1)) - nt(seen, right_nt(rights[n]))
        table[here, here] = jnp.where(row >= col, inside, NEGATIVE)
        moving[here, :] = left(start)
    for m in range(blocks - 2, -1, -1):
        here = pl.ds(m * C, C)
        after = pl.ds((m + 1) * C, (blocks - 1 - m) * C)
        rows = moving[after, :]
        table[after, here] = nt(rows, right_nt(finals[here, :]))
        moving[after, :] = left(nn(rows, right_nn(passages[m])))
    moved[...] = moving[...]
    for n in range(blocks):
        here = pl.ds(n * C, C)
        upto = pl.ds(0, (n + 1) * C)
        s = table[here, upto]
        m = jnp.max(s, axis=1, keepdims=True)
        p = jnp.exp2(s - m)
        peak[here, :] = jnp.broadcast_to(m, (C, C))
        total[here, :] = jnp.broadcast_to(jnp.sum(p, axis=1, keepdims=True), (C, C))
        summed[here, :] = jnp.dot(p.astype(BF16), values[upto, :], preferred_element_type=F32)


def own(queries, keys, values, passages, inverses, rights, finals, unit):
    rows = queries.shape[0]
    flat = jax.ShapeDtypeStruct((rows, C), F32)
    return pl.pallas_call(
        own_kernel,
        out_shape=(jax.ShapeDtypeStruct((rows, 2 * C), BF16), flat, flat, flat),
        scratch_shapes=[pltpu.VMEM((rows, rows), F32), pltpu.VMEM((rows, 2 * C), BF16)],
        compiler_params=pltpu.CompilerParams(vmem_limit_bytes=VMEM_LIMIT),
        name="own",
    )(queries, keys, values, passages, inverses, rights, finals, unit)


ROWS = 256


def earlier_kernel(number, moved, peak, total, summed, all_keys, all_values, out, mv, mx, ls, acc):
    rows = moved.shape[0]
    mv[...] = moved[...]
    mx[...] = peak[...]
    ls[...] = total[...]
    acc[...] = summed[...]
    here_number = number[0]

    def visit(step, carry):
        source = here_number - 1 - step
        k = all_keys[source, pl.ds(0, rows), :]
        k2 = jnp.concatenate([k, k], axis=1)
        v = all_values[source]
        high = all_keys[source, pl.ds(rows, C), :]
        low = all_keys[source, pl.ds(rows + C, C), :]
        pair = jnp.concatenate([high, low], axis=1)
        step_by = jnp.concatenate([pair, pair], axis=0)
        for b in range(rows // ROWS):
            here = pl.ds(b * ROWS, ROWS)
            q = mv[here, :]
            s = contract_last(q, k2)
            mv[here, :] = left(nn(q, step_by))
            old = mx[here, :]
            new = jnp.maximum(old, jnp.max(s, axis=1, keepdims=True))
            mx[here, :] = new
            shrink = jnp.exp2(old - new)
            p = jnp.exp2(s - jnp.tile(new, (1, rows // C)))
            ls[here, :] = ls[here, :] * shrink + jnp.sum(p, axis=1, keepdims=True)
            acc[here, :] = acc[here, :] * shrink + jnp.dot(p.astype(BF16), v, preferred_element_type=F32)
        return carry

    lax.fori_loop(0, here_number, visit, 0)
    out[...] = (acc[...] / ls[...]).astype(BF16)


def earlier(number, moved, peak, total, summed, all_keys, all_values):
    rows = moved.shape[0]
    vmem = pl.BlockSpec(memory_space=pltpu.VMEM)
    return pl.pallas_call(
        earlier_kernel,
        out_shape=jax.ShapeDtypeStruct((rows, C), BF16),
        in_specs=[pl.BlockSpec(memory_space=pltpu.SMEM)] + [vmem] * 6,
        out_specs=vmem,
        scratch_shapes=[
            pltpu.VMEM((rows, 2 * C), BF16),
            pltpu.VMEM((rows, C), F32),
            pltpu.VMEM((rows, C), F32),
            pltpu.VMEM((rows, C), F32),
        ],
        compiler_params=pltpu.CompilerParams(vmem_limit_bytes=VMEM_LIMIT),
        name="earlier",
    )(number, moved, peak, total, summed, all_keys, all_values)


def over_heads(x):
    by_z = [lax.ppermute(x, "head", [(i, (i + 2 * s) % 8) for i in range(8)]) for s in (1, 3, 2)]
    return by_z


def body(queries, keys, values, house, rates, out_weight):
    rows = queries.shape[0]
    blocks = rows // C
    number = lax.axis_index("ctx")
    q, k, v, h = (x[:, 0, :] for x in (queries, keys, values, house))
    sent, passages, inverses, rights, finals, unit = transport(k, h, rates.reshape(blocks, C))
    all_values = lax.all_gather(v, "ctx", axis=0)
    all_keys = lax.all_gather(sent, "ctx", axis=0)
    moved, peak, total, summed = own(q, k, v, passages, inverses, rights, finals, unit)
    attended = earlier(number.astype(jnp.int32)[None], moved, peak, total, summed, all_keys, all_values)
    columns = lax.all_to_all(out_weight, "head", split_axis=1, concat_axis=0, tiled=True)
    everyone = lax.all_to_all(
        jnp.broadcast_to(attended[None], (8, *attended.shape)), "head", 0, 0, tiled=True
    )
    flattened = jnp.moveaxis(everyone, 0, 1).reshape(rows, 8 * C)
    projected = jnp.dot(flattened, columns, preferred_element_type=F32)
    return (attended[:, None, :], projected.astype(BF16))


def solution(mesh):
    in_specs = (
        P("ctx", "head", None),
        P("ctx", "head", None),
        P("ctx", "head", None),
        P("ctx", "head", None),
        P("head", "ctx"),
        P("head", None),
    )
    out_specs = (P("ctx", "head", None), P("ctx", "head"))
    return jax.shard_map(body, mesh=mesh, in_specs=in_specs, out_specs=out_specs, check_vma=False)
```

```python
import jax
import jax.numpy as jnp
from jax import lax
from jax.experimental import pallas as pl
from jax.experimental.pallas import tpu as pltpu
from jax.sharding import PartitionSpec as P

C = 128
F32 = jnp.float32
BF16 = jnp.bfloat16
EPSILON = 1e-06
NEGATIVE = -1e30
LOG2E = 1.4426950408889634
VMEM_LIMIT = 56 * 1024 * 1024


def split(x):
    high = x.astype(BF16)
    return high, (x - high.astype(F32)).astype(BF16)


def left(x):
    return jnp.concatenate(split(x), axis=1)


def right_nn(x):
    pair = jnp.concatenate(split(x), axis=1)
    return jnp.concatenate([pair, pair], axis=0)


def right_nt(x):
    high, low = split(x)
    return jnp.concatenate(
        [jnp.concatenate([high, high], axis=1), jnp.concatenate([low, low], axis=1)], axis=0
    )


def halves(x):
    return x[:, : x.shape[1] // 2] + x[:, x.shape[1] // 2 :]


def nn(a, b):
    return halves(jnp.dot(a, b, preferred_element_type=F32))


def contract_last(a, b):
    return lax.dot_general(a, b, (((1,), (1,)), ((), ())), preferred_element_type=F32)


def nt(a, b):
    return halves(contract_last(a, b))


def unit_house(house):
    raw = house.astype(F32)
    return raw / jnp.sqrt(jnp.sum(raw * raw, axis=1, keepdims=True) + EPSILON)


def transport_kernel(keys, house, rates, sent, passages, inverses, rights, finals, unit):
    blocks = rates.shape[0]
    row = lax.broadcasted_iota(jnp.int32, (C, C), 0)
    col = lax.broadcasted_iota(jnp.int32, (C, C), 1)
    eye = jnp.where(row == col, 1.0, 0.0).astype(F32)
    every = range(blocks)
    w = [unit_house(house[pl.ds(n * C, C), :]) for n in every]
    for n in every:
        unit[pl.ds(n * C, C), :] = w[n]
    wl = [left(x) for x in w]
    strict = []
    for n in every:
        gram = nt(wl[n], right_nt(w[n]))
        decay = jnp.transpose(jnp.broadcast_to(rates[n : n + 1, :], (C, C)))
        strict.append(jnp.where(row > col, gram, 0.0) * decay)
    x = [eye - jnp.where((row // 2) == (col // 2), strict[n], 0.0) for n in every]
    size = 2
    while size < C:
        band = ((row // (2 * size)) == (col // (2 * size))) & ((row // size) != (col // size))
        inner = [nn(left(jnp.where(band, strict[n], 0.0)), right_nn(x[n])) for n in every]
        x = [x[n] - nn(left(x[n]), right_nn(inner[n])) for n in every]
        size *= 2
    t = [x[n] * rates[n : n + 1, :] for n in every]
    for n in every:
        inverses[n] = t[n]
    final = []
    for n in every:
        k = keys[pl.ds(n * C, C), :]
        met = jnp.where(col > row, contract_last(jnp.concatenate([k, k], axis=1), wl[n]), 0.0)
        r = nt(left(met), right_nt(t[n]))
        rights[n] = r
        f = k.astype(F32) - nn(left(r), right_nn(w[n]))
        finals[pl.ds(n * C, C), :] = f
        final.append(f)
    passage = []
    for n in every:
        u = nn(left(t[n]), right_nn(w[n]))
        passage.append(eye - nn(left(jnp.transpose(w[n])), right_nn(u)))
        passages[n] = passage[n]
    sent[pl.ds((blocks - 1) * C, C), :] = final[blocks - 1].astype(BF16)
    s = passage[blocks - 1]
    for n in range(blocks - 2, -1, -1):
        sent[pl.ds(n * C, C), :] = nt(left(final[n]), right_nt(s)).astype(BF16)
        s = nn(left(s), right_nn(passage[n]))
    high, low = split(s)
    sent[pl.ds(blocks * C, C), :] = high
    sent[pl.ds((blocks + 1) * C, C), :] = low


def transport(keys, house, rates):
    rows = keys.shape[0]
    blocks = rows // C
    square = jax.ShapeDtypeStruct((blocks, C, C), F32)
    flat = jax.ShapeDtypeStruct((rows, C), F32)
    return pl.pallas_call(
        transport_kernel,
        out_shape=(jax.ShapeDtypeStruct((rows + 2 * C, C), BF16), square, square, square, flat, flat),
        compiler_params=pltpu.CompilerParams(vmem_limit_bytes=VMEM_LIMIT),
        name="transport",
    )(keys, house, rates)


def own_kernel(
    queries, keys, values, passages, inverses, rights, finals, unit, moved, peak, total, summed, table, moving
):
    blocks = passages.shape[0]
    row = lax.broadcasted_iota(jnp.int32, (C, C), 0)
    col = lax.broadcasted_iota(jnp.int32, (C, C), 1)
    for n in range(blocks):
        here = pl.ds(n * C, C)
        q = queries[here, :].astype(F32) * (C**-0.5 * LOG2E)
        w = unit[here, :]
        k = keys[here, :]
        ql = left(q)
        seen = left(jnp.where(row >= col, nt(ql, right_nt(w)), 0.0))
        start = q - nn(left(nn(seen, right_nn(inverses[n]))), right_nn(w))
        inside = contract_last(ql, jnp.concatenate([k, k], axis=1)) - nt(seen, right_nt(rights[n]))
        table[here, here] = jnp.where(row >= col, inside, NEGATIVE)
        moving[here, :] = left(start)
    for m in range(blocks - 2, -1, -1):
        here = pl.ds(m * C, C)
        after = pl.ds((m + 1) * C, (blocks - 1 - m) * C)
        rows = moving[after, :]
        table[after, here] = nt(rows, right_nt(finals[here, :]))
        moving[after, :] = left(nn(rows, right_nn(passages[m])))
    moved[...] = moving[...]
    for n in range(blocks):
        here = pl.ds(n * C, C)
        upto = pl.ds(0, (n + 1) * C)
        s = table[here, upto]
        m = jnp.max(s, axis=1, keepdims=True)
        p = jnp.exp2(s - m)
        peak[here, :] = jnp.broadcast_to(m, (C, C))
        total[here, :] = jnp.broadcast_to(jnp.sum(p, axis=1, keepdims=True), (C, C))
        summed[here, :] = jnp.dot(p.astype(BF16), values[upto, :], preferred_element_type=F32)


def own(queries, keys, values, passages, inverses, rights, finals, unit):
    rows = queries.shape[0]
    flat = jax.ShapeDtypeStruct((rows, C), F32)
    return pl.pallas_call(
        own_kernel,
        out_shape=(jax.ShapeDtypeStruct((rows, 2 * C), BF16), flat, flat, flat),
        scratch_shapes=[pltpu.VMEM((rows, rows), F32), pltpu.VMEM((rows, 2 * C), BF16)],
        compiler_params=pltpu.CompilerParams(vmem_limit_bytes=VMEM_LIMIT),
        name="own",
    )(queries, keys, values, passages, inverses, rights, finals, unit)


ROWS = 256
SIDE = 4
LSE_ROWS = 32


def stacked(pair):
    return jnp.concatenate([pair, pair], axis=0)


def fetch_row(y, keys, values, key_row, value_row, sems):
    copies = []
    for d in range(SIDE):
        slot = lax.rem(y + (SIDE - d), SIDE)
        copies.append(pltpu.make_async_copy(keys[d], key_row.at[slot], sems.at[0, d]))
        copies.append(pltpu.make_async_copy(values[d], value_row.at[slot], sems.at[1, d]))
    for copy in copies:
        copy.start()
    for copy in copies:
        copy.wait()


def visit_row(first, count, key_row, value_row, mv, mx, ls, acc):
    rows = mv.shape[0]

    def visit(step, carry):
        source = first - step
        k = key_row[source, pl.ds(0, rows), :]
        k2 = jnp.concatenate([k, k], axis=1)
        v = value_row[source]
        high = key_row[source, pl.ds(rows, C), :]
        low = key_row[source, pl.ds(rows + C, C), :]
        step_by = stacked(jnp.concatenate([high, low], axis=1))
        for b in range(rows // ROWS):
            here = pl.ds(b * ROWS, ROWS)
            q = mv[here, :]
            s = contract_last(q, k2)
            mv[here, :] = left(nn(q, step_by))
            old = mx[here, :]
            new = jnp.maximum(old, jnp.max(s, axis=1, keepdims=True))
            mx[here, :] = new
            shrink = jnp.exp2(old - new)
            p = jnp.exp2(s - jnp.tile(new, (1, rows // C)))
            ls[here, :] = ls[here, :] * shrink + jnp.sum(p, axis=1, keepdims=True)
            acc[here, :] = acc[here, :] * shrink + jnp.dot(p.astype(BF16), v, preferred_element_type=F32)
        return carry

    lax.fori_loop(0, count, visit, 0)


def row_scratch(rows, tail):
    return [
        pltpu.VMEM((SIDE, rows + 2 * C, C), BF16),
        pltpu.VMEM((SIDE, rows, C), BF16),
        pltpu.SemaphoreType.DMA((2, SIDE)),
        pltpu.VMEM((rows, 2 * C), BF16),
    ] + tail


ANY = pl.BlockSpec(memory_space=pl.ANY)
SCALARS = pl.BlockSpec(memory_space=pltpu.SMEM)
WHOLE = pl.BlockSpec(memory_space=pltpu.VMEM)


def chain_kernel(place, k0, k1, k2, k3, out, steps, sems):
    y = place[1]
    rows = k0.shape[0] - 2 * C
    copies = []
    for d, k in enumerate((k0, k1, k2, k3)):
        slot = lax.rem(y + (SIDE - d), SIDE)
        copies.append(pltpu.make_async_copy(k.at[pl.ds(rows, 2 * C)], steps.at[slot], sems.at[d]))
    for copy in copies:
        copy.start()
    for copy in copies:
        copy.wait()
    row = lax.broadcasted_iota(jnp.int32, (C, C), 0)
    col = lax.broadcasted_iota(jnp.int32, (C, C), 1)

    def pair(n):
        return jnp.concatenate([steps[n, pl.ds(0, C), :], steps[n, pl.ds(C, C), :]], axis=1)

    def advance(step, so_far):
        return nn(left(so_far), stacked(pair(y - 1 - step)))

    before = lax.fori_loop(0, y, advance, jnp.where(row == col, 1.0, 0.0).astype(F32))
    out[pl.ds(0, C), :] = left(before)
    whole = pair(SIDE - 1)
    for n in range(SIDE - 2, -1, -1):
        whole = left(nn(whole, stacked(pair(n))))
    out[pl.ds(C, C), :] = whole


def chain(place, keys):
    return pl.pallas_call(
        chain_kernel,
        out_shape=jax.ShapeDtypeStruct((2 * C, 2 * C), BF16),
        in_specs=[SCALARS] + [ANY] * SIDE,
        out_specs=WHOLE,
        scratch_shapes=[pltpu.VMEM((SIDE, 2 * C, C), BF16), pltpu.SemaphoreType.DMA((SIDE,))],
        compiler_params=pltpu.CompilerParams(vmem_limit_bytes=VMEM_LIMIT),
        name="chain",
    )(place, *keys)


def row_kernel(
    place, moved, peak, total, summed, k0, k1, k2, k3, v0, v1, v2, v3, mx, ls, acc, key_row, value_row, sems, mv
):
    y = place[1]
    mv[...] = moved[...]
    mx[...] = peak[...]
    ls[...] = total[...]
    acc[...] = summed[...]

    @pl.when(y > 0)
    def _():
        fetch_row(y, (k0, k1, k2, k3), (v0, v1, v2, v3), key_row, value_row, sems)
        visit_row(y - 1, y, key_row, value_row, mv, mx, ls, acc)


def row(place, moved, peak, total, summed, keys, values):
    rows = moved.shape[0]
    flat = jax.ShapeDtypeStruct((rows, C), F32)
    return pl.pallas_call(
        row_kernel,
        out_shape=(flat, flat, flat),
        in_specs=[SCALARS] + [WHOLE] * 4 + [ANY] * (2 * SIDE),
        out_specs=(WHOLE, WHOLE, WHOLE),
        scratch_shapes=row_scratch(rows, []),
        compiler_params=pltpu.CompilerParams(vmem_limit_bytes=VMEM_LIMIT),
        name="row",
    )(place, moved, peak, total, summed, *keys, *values)


def visitor_kernel(*refs):
    place, query, k0, k1, k2, k3, v0, v1, v2, v3 = refs[:10]
    key_row, value_row, sems, mv, mx, ls, acc = refs[-7:]
    out = refs[-8]
    chains = refs[10:-8]
    distance = len(chains)
    y = place[1]
    rows = mv.shape[0]

    @pl.when(place[0] + distance < SIDE)
    def _():
        fetch_row(y, (k0, k1, k2, k3), (v0, v1, v2, v3), key_row, value_row, sems)
        along = chains[-1][pl.ds(0, C), :]
        for link in chains[-2::-1]:
            along = left(nn(along, stacked(link[pl.ds(C, C), :])))
        mv[...] = left(nn(query[...], stacked(along)))
        mx[...] = jnp.full(mx.shape, NEGATIVE, F32)
        ls[...] = jnp.zeros(ls.shape, F32)
        acc[...] = jnp.zeros(acc.shape, F32)
        visit_row(SIDE - 1, SIDE, key_row, value_row, mv, mx, ls, acc)
        out[pl.ds(0, rows), :] = (acc[...] / ls[...]).astype(BF16)
        lines = []
        for n in range(rows // C):
            here = pl.ds(n * C, C)
            lines.append(jnp.transpose(mx[here, :] + jnp.log2(ls[here, :]))[0:1, :])
        lse = jnp.concatenate(lines, axis=0)
        high = lse.astype(BF16).astype(F32)
        middle = (lse - high).astype(BF16).astype(F32)
        low = lse - high - middle
        out[pl.ds(rows, LSE_ROWS), :] = jnp.concatenate(
            [high, middle, low, jnp.zeros_like(lse)], axis=0
        ).astype(BF16)


def visitor(place, query, keys, values, chains):
    rows = query.shape[0]
    return pl.pallas_call(
        visitor_kernel,
        out_shape=jax.ShapeDtypeStruct((rows + LSE_ROWS, C), BF16),
        in_specs=[SCALARS, WHOLE] + [ANY] * (2 * SIDE) + [WHOLE] * len(chains),
        out_specs=WHOLE,
        scratch_shapes=row_scratch(rows, [pltpu.VMEM((rows, C), F32)] * 3),
        compiler_params=pltpu.CompilerParams(vmem_limit_bytes=VMEM_LIMIT),
        name="visitor",
    )(place, query, *keys, *values, *chains)


def merge_kernel(place, mx, ls, acc, r1, r2, r3, out):
    rows = mx.shape[0]
    lines = []
    for d, r in enumerate((r1, r2, r3)):
        tail = r[pl.ds(rows, LSE_ROWS), :].astype(F32)
        blocks = rows // C
        lse = tail[0:blocks] + tail[blocks : 2 * blocks] + tail[2 * blocks : 3 * blocks]
        lines.append(jnp.where(place[0] > d, lse, NEGATIVE))
    for n in range(rows // C):
        here = pl.ds(n * C, C)
        lse = [jnp.transpose(jnp.broadcast_to(line[n : n + 1, :], (C, C))) for line in lines]
        top = mx[here, :]
        for one in lse:
            top = jnp.maximum(top, one)
        share = jnp.exp2(mx[here, :] - top)
        total = ls[here, :] * share
        summed = acc[here, :] * share
        for d, r in enumerate((r1, r2, r3)):
            share = jnp.exp2(lse[d] - top)
            total += share
            summed += jnp.where(place[0] > d, share * r[here, :].astype(F32), 0.0)
        out[here, :] = (summed / total).astype(BF16)


def merge(place, mx, ls, acc, returned):
    rows = mx.shape[0]
    return pl.pallas_call(
        merge_kernel,
        out_shape=jax.ShapeDtypeStruct((rows, C), BF16),
        in_specs=[SCALARS] + [WHOLE] * 6,
        out_specs=WHOLE,
        compiler_params=pltpu.CompilerParams(vmem_limit_bytes=VMEM_LIMIT),
        name="merge",
    )(place, mx, ls, acc, *returned)


def project_kernel(place, here, there, columns, *rest):
    out = rest[-1]
    z, core = place[2], place[3]
    total = None
    for s in range(SIDE):
        chip = lax.rem(z + (SIDE - s), SIDE)
        x = jnp.concatenate([here[s], there[s]], axis=1)
        w = jnp.concatenate([columns[2 * chip + core], columns[2 * chip + 1 - core]], axis=0)
        part = jnp.dot(x, w, preferred_element_type=F32)
        total = part if total is None else total + part
    out[...] = total.astype(BF16)


def project(place, here, there, columns, part, parts, so_far):
    rows = here.shape[1]
    width = columns.shape[2]
    tile = 256
    steps = rows // tile
    extra = [] if so_far is None else [so_far]
    piece = pl.BlockSpec((SIDE, tile, C), lambda i: (0, i, 0))
    return pl.pallas_call(
        project_kernel,
        out_shape=jax.ShapeDtypeStruct((rows * parts, width), BF16),
        grid=(steps,),
        in_specs=[SCALARS, piece, piece, WHOLE] + [ANY] * len(extra),
        out_specs=pl.BlockSpec((tile, width), lambda i: (part * steps + i, 0)),
        input_output_aliases={4: 0} if extra else {},
        compiler_params=pltpu.CompilerParams(vmem_limit_bytes=VMEM_LIMIT),
        name="project",
    )(place, here, there, columns, *extra)


def along_y(x, d):
    return lax.ppermute(x, "ctx", [(i, i - i % SIDE + (i + d) % SIDE) for i in range(SIDE * SIDE)])


def down_x(x, d):
    return lax.ppermute(x, "ctx", [(i, i - SIDE * d) for i in range(SIDE * d, SIDE * SIDE)])


def up_x(x, d):
    return lax.ppermute(x, "ctx", [(i, i + SIDE * d) for i in range(SIDE * SIDE - SIDE * d)])


def along_z(x, d):
    return lax.ppermute(x, "head", [(i, (i + 2 * d) % (2 * SIDE)) for i in range(2 * SIDE)])


def other_core(x):
    return lax.ppermute(x, "head", [(i, i ^ 1) for i in range(2 * SIDE)])


PARTS = 2


def body(queries, keys, values, house, rates, out_weight):
    rows = queries.shape[0]
    blocks = rows // C
    number = lax.axis_index("ctx")
    head = lax.axis_index("head")
    place = jnp.stack([number // SIDE, number % SIDE, head // 2, head % 2]).astype(jnp.int32)
    q, k, v, h = (x[:, 0, :] for x in (queries, keys, values, house))
    row_values = [v] + [along_y(v, d) for d in (1, 2, 3)]
    sent, passages, inverses, rights, finals, unit = transport(k, h, rates.reshape(blocks, C))
    row_keys = [sent] + [along_y(sent, d) for d in (1, 2, 3)]
    moved, peak, total, summed = own(q, k, v, passages, inverses, rights, finals, unit)
    visiting = [down_x(moved, d) for d in (1, 2, 3)]
    links = chain(place, row_keys)
    links = [down_x(links, d) for d in (1, 2, 3)]
    mx, ls, acc = row(place, moved, peak, total, summed, row_keys, row_values)
    returned = []
    for d in (1, 2, 3):
        partial = visitor(place, visiting[d - 1], row_keys, row_values, links[:d])
        returned.append(up_x(partial, d))
    attended = merge(place, mx, ls, acc, returned)
    width = out_weight.shape[1] // (2 * SIDE)
    columns = lax.all_to_all(out_weight, "head", split_axis=1, concat_axis=0, tiled=True)
    columns = columns.reshape(2 * SIDE, C, width)
    projected = None
    pieces = []
    for part in range(PARTS):
        size = rows // PARTS
        mine = attended[part * size : (part + 1) * size]
        here = jnp.stack([mine] + [along_z(mine, d) for d in (1, 2, 3)])
        pieces.append((here, other_core(here)))
    for part, (here, there) in enumerate(pieces):
        projected = project(place, here, there, columns, part, PARTS, projected)
    return (attended[:, None, :], projected)


def solution(mesh):
    in_specs = (
        P("ctx", "head", None),
        P("ctx", "head", None),
        P("ctx", "head", None),
        P("ctx", "head", None),
        P("head", "ctx"),
        P("head", None),
    )
    out_specs = (P("ctx", "head", None), P("ctx", "head"))
    return jax.shard_map(body, mesh=mesh, in_specs=in_specs, out_specs=out_specs, check_vma=False)
```

```python
import jax
import jax.numpy as jnp
from jax import lax
from jax.experimental import pallas as pl
from jax.experimental.pallas import tpu as pltpu
from jax.sharding import PartitionSpec as P

C = 128
F32 = jnp.float32
BF16 = jnp.bfloat16
EPSILON = 1e-06
NEGATIVE = -1e30
LOG2E = 1.4426950408889634
VMEM_LIMIT = 56 * 1024 * 1024


def cost(microseconds):
    return pl.CostEstimate(flops=int(microseconds * 1.15e9), transcendentals=0, bytes_accessed=2**20)


def stacked(pair):
    return jnp.concatenate([pair, pair], axis=0)


def split(x):
    high = x.astype(BF16)
    return high, (x - high.astype(F32)).astype(BF16)


def left(x):
    return jnp.concatenate(split(x), axis=1)


def right_nn(x):
    pair = jnp.concatenate(split(x), axis=1)
    return jnp.concatenate([pair, pair], axis=0)


def right_nt(x):
    high, low = split(x)
    return jnp.concatenate(
        [jnp.concatenate([high, high], axis=1), jnp.concatenate([low, low], axis=1)], axis=0
    )


def halves(x):
    return x[:, : x.shape[1] // 2] + x[:, x.shape[1] // 2 :]


def nn(a, b):
    return halves(jnp.dot(a, b, preferred_element_type=F32))


def contract_last(a, b):
    return lax.dot_general(a, b, (((1,), (1,)), ((), ())), preferred_element_type=F32)


def nt(a, b):
    return halves(contract_last(a, b))


def unit_house(house):
    raw = house.astype(F32)
    return raw / jnp.sqrt(jnp.sum(raw * raw, axis=1, keepdims=True) + EPSILON)


def transport_kernel(keys, values, house, rates, step, sent, passages, prefixes, applied, rights, finals, unit):
    rows = keys.shape[0]
    sent[pl.ds(rows, rows), :] = values[...]
    blocks = rates.shape[0]
    row = lax.broadcasted_iota(jnp.int32, (C, C), 0)
    col = lax.broadcasted_iota(jnp.int32, (C, C), 1)
    eye = jnp.where(row == col, 1.0, 0.0).astype(F32)
    every = range(blocks)
    w = [unit_house(house[pl.ds(n * C, C), :]) for n in every]
    for n in every:
        unit[pl.ds(n * C, C), :] = w[n]
    wl = [left(x) for x in w]
    strict = []
    for n in every:
        gram = nt(wl[n], right_nt(w[n]))
        decay = jnp.transpose(jnp.broadcast_to(rates[n : n + 1, :], (C, C)))
        strict.append(jnp.where(row > col, gram, 0.0) * decay)
    x = [eye - jnp.where((row // 2) == (col // 2), strict[n], 0.0) for n in every]
    size = 2
    while size < C:
        band = ((row // (2 * size)) == (col // (2 * size))) & ((row // size) != (col // size))
        inner = [nn(left(jnp.where(band, strict[n], 0.0)), right_nn(x[n])) for n in every]
        x = [x[n] - nn(left(x[n]), right_nn(inner[n])) for n in every]
        size *= 2
    t = [x[n] * rates[n : n + 1, :] for n in every]
    final = []
    for n in every:
        k = keys[pl.ds(n * C, C), :]
        met = jnp.where(col > row, contract_last(jnp.concatenate([k, k], axis=1), wl[n]), 0.0)
        r = nt(left(met), right_nt(t[n]))
        rights[n] = r
        f = k.astype(F32) - nn(left(r), right_nn(w[n]))
        finals[pl.ds(n * C, C), :] = f
        final.append(f)
    passage = []
    for n in every:
        u = nn(left(t[n]), right_nn(w[n]))
        applied[n] = u
        passage.append(eye - nn(left(jnp.transpose(w[n])), right_nn(u)))
        passages[n] = passage[n]
    sent[pl.ds((blocks - 1) * C, C), :] = final[blocks - 1].astype(BF16)
    s = passage[blocks - 1]
    a = passage[0]
    prefixes[0] = left(eye)
    for n in range(blocks - 2, -1, -1):
        prefixes[blocks - 1 - n] = left(a)
        if n:
            a = nn(left(passage[blocks - 1 - n]), right_nn(a))
        sent[pl.ds(n * C, C), :] = nt(left(final[n]), right_nt(s)).astype(BF16)
        s = nn(left(s), right_nn(passage[n]))
    step[...] = left(s)


def transport(keys, values, house, rates):
    rows = keys.shape[0]
    blocks = rows // C
    square = jax.ShapeDtypeStruct((blocks, C, C), F32)
    flat = jax.ShapeDtypeStruct((rows, C), F32)
    return pl.pallas_call(
        transport_kernel,
        out_shape=(
            jax.ShapeDtypeStruct((C, 2 * C), BF16),
            jax.ShapeDtypeStruct((2 * rows, C), BF16),
            square,
            jax.ShapeDtypeStruct((blocks, C, 2 * C), BF16),
            square,
            square,
            flat,
            flat,
        ),
        cost_estimate=cost(8),
        compiler_params=pltpu.CompilerParams(vmem_limit_bytes=VMEM_LIMIT),
        name="transport",
    )(keys, values, house, rates)


SIDE = 4
COST_LEAD = 3
COST_OWN = 5
COST_DEAL = 2
COST_VISIT = 7
COST_ROW = 6


def lead_kernel(place, queries, prefixes, applied, unit, t0, t1, t2, t3, leaving, suffixes, seens, starts, along, steps):
    blocks = applied.shape[0]
    rows = queries.shape[0]
    y = place[1]
    row = lax.broadcasted_iota(jnp.int32, (C, C), 0)
    col = lax.broadcasted_iota(jnp.int32, (C, C), 1)
    eye = jnp.where(row == col, 1.0, 0.0).astype(F32)
    along[...] = left(eye)
    for d, t in enumerate((t0, t1, t2, t3)):
        steps[lax.rem(y + (SIDE - d), SIDE)] = t[...]
        if d:

            @pl.when(y >= d)
            def _(t=t):
                along[...] = left(nn(along[...], stacked(t[...])))

    suffix = left(eye)
    for n in range(SIDE - 1, -1, -1):
        suffixes[lax.rem(y + (SIDE - n), SIDE)] = suffix
        suffix = left(nn(suffix, stacked(steps[n])))
    move = stacked(along[...])
    for n in range(blocks):
        here = pl.ds(n * C, C)
        q = queries[here, :].astype(F32) * (C**-0.5 * LOG2E)
        seen = left(jnp.where(row >= col, nt(left(q), right_nt(unit[here, :])), 0.0))
        start = left(q - nn(seen, right_nn(applied[n])))
        seens[here, :] = seen
        starts[here, :] = start
        out = left(nn(start, stacked(left(nn(prefixes[n], move)))))
        leaving[here, :] = out
    leaving[pl.ds(rows, C), :] = suffix


def lead(place, queries, prefixes, applied, unit, steps):
    rows = queries.shape[0]
    pair = jax.ShapeDtypeStruct((rows, 2 * C), BF16)
    return pl.pallas_call(
        lead_kernel,
        out_shape=(
            jax.ShapeDtypeStruct((rows + C, 2 * C), BF16),
            jax.ShapeDtypeStruct((SIDE, C, 2 * C), BF16),
            pair,
            pair,
        ),
        in_specs=[SCALARS] + [WHOLE] * (4 + SIDE),
        out_specs=(WHOLE,) * 4,
        scratch_shapes=[pltpu.VMEM((C, 2 * C), BF16), pltpu.VMEM((SIDE, C, 2 * C), BF16)],
        compiler_params=pltpu.CompilerParams(vmem_limit_bytes=VMEM_LIMIT),
        cost_estimate=cost(COST_LEAD),
        name="lead",
    )(place, queries, prefixes, applied, unit, *steps)


def own_kernel(queries, keys, values, seens, starts, passages, rights, finals, moved, peak, total, summed, table):
    blocks = passages.shape[0]
    row = lax.broadcasted_iota(jnp.int32, (C, C), 0)
    col = lax.broadcasted_iota(jnp.int32, (C, C), 1)
    for n in range(blocks):
        here = pl.ds(n * C, C)
        q = queries[here, :].astype(F32) * (C**-0.5 * LOG2E)
        k = keys[here, :]
        inside = contract_last(left(q), jnp.concatenate([k, k], axis=1)) - nt(seens[here, :], right_nt(rights[n]))
        table[here, here] = jnp.where(row >= col, inside, NEGATIVE)
        moved[here, :] = starts[here, :]
    for m in range(blocks - 2, -1, -1):
        here = pl.ds(m * C, C)
        after = pl.ds((m + 1) * C, (blocks - 1 - m) * C)
        block_rows = moved[after, :]
        table[after, here] = nt(block_rows, right_nt(finals[here, :]))
        moved[after, :] = left(nn(block_rows, right_nn(passages[m])))
    for n in range(blocks):
        here = pl.ds(n * C, C)
        upto = pl.ds(0, (n + 1) * C)
        s = table[here, upto]
        m = jnp.max(s, axis=1, keepdims=True)
        p = jnp.exp2(s - m)
        peak[here, :] = jnp.broadcast_to(m, (C, C))
        total[here, :] = jnp.broadcast_to(jnp.sum(p, axis=1, keepdims=True), (C, C))
        summed[here, :] = jnp.dot(p.astype(BF16), values[upto, :], preferred_element_type=F32)


def own(queries, keys, values, seens, starts, passages, rights, finals):
    rows = values.shape[0]
    flat = jax.ShapeDtypeStruct((rows, C), F32)
    return pl.pallas_call(
        own_kernel,
        out_shape=(jax.ShapeDtypeStruct((rows, 2 * C), BF16), flat, flat, flat),
        scratch_shapes=[pltpu.VMEM((rows, rows), F32)],
        compiler_params=pltpu.CompilerParams(vmem_limit_bytes=VMEM_LIMIT),
        cost_estimate=cost(COST_OWN),
        name="own",
    )(queries, keys, values, seens, starts, passages, rights, finals)


ROWS = 512
LSE_ROWS = 32
ANY = pl.BlockSpec(memory_space=pl.ANY)
SCALARS = pl.BlockSpec(memory_space=pltpu.SMEM)
WHOLE = pl.BlockSpec(memory_space=pltpu.VMEM)


def meet(q, keys, values, state):
    rows = keys.shape[0]
    k = keys[...]
    v = values[...]
    s = contract_last(q, jnp.concatenate([k, k], axis=1))
    top = jnp.max(s, axis=1, keepdims=True)
    if state is None:
        new = jnp.broadcast_to(top, (q.shape[0], C))
    else:
        new = jnp.maximum(state[0], top)
    p = jnp.exp2(s - jnp.tile(new, (1, rows // C))).astype(BF16)
    pv = jnp.dot(p, jnp.concatenate([v, jnp.ones_like(v)], axis=1), preferred_element_type=F32)
    if state is None:
        return new, pv[:, C:], pv[:, :C]
    shrink = jnp.exp2(state[0] - new)
    return new, state[1] * shrink + pv[:, C:], state[2] * shrink + pv[:, :C]


def row_kernel(place, moved, peak, total, summed, t1, t2, s1, k2, v2, s3, mx, ls, acc, mv):
    y = place[1]
    rows = moved.shape[0]
    mv[...] = moved[...]
    mx[...] = peak[...]
    ls[...] = total[...]
    acc[...] = summed[...]
    halves_of = lambda s: (s.at[pl.ds(0, rows)], s.at[pl.ds(rows, rows)])
    for d, (t, shard) in enumerate(((t1, halves_of(s1)), (t2, (k2, v2)), (None, halves_of(s3)))):

        @pl.when(y > d)
        def _(t=t, shard=shard):
            for b in range(rows // ROWS):
                here = pl.ds(b * ROWS, ROWS)
                q = mv[here, :]
                mx[here, :], ls[here, :], acc[here, :] = meet(
                    q, *shard, (mx[here, :], ls[here, :], acc[here, :])
                )
                if t is not None:
                    mv[here, :] = left(nn(q, stacked(t[...])))


def row(place, moved, peak, total, summed, steps, shards):
    rows = moved.shape[0]
    flat = jax.ShapeDtypeStruct((rows, C), F32)
    return pl.pallas_call(
        row_kernel,
        out_shape=(flat, flat, flat),
        in_specs=[SCALARS] + [WHOLE] * 10,
        out_specs=(WHOLE, WHOLE, WHOLE),
        scratch_shapes=[pltpu.VMEM((rows, 2 * C), BF16)],
        compiler_params=pltpu.CompilerParams(vmem_limit_bytes=VMEM_LIMIT),
        cost_estimate=cost(COST_ROW),
        name="row",
    )(place, moved, peak, total, summed, steps[1], steps[2], *shards[1:])


def visitors_kernel(place, q1, q2, q3, suffixes, s0, s1, k2, v2, s3, *rest, distances):
    queries = (q1, q2, q3)
    outs = rest[: len(distances)]
    mx, ls, acc, along = rest[len(distances) :]
    rows = mx.shape[0]
    shards = [(s.at[pl.ds(0, rows)], s.at[pl.ds(rows, rows)]) for s in (s0, s1, s3)]
    shards.insert(2, (k2, v2))
    row = lax.broadcasted_iota(jnp.int32, (C, C), 0)
    col = lax.broadcasted_iota(jnp.int32, (C, C), 1)
    for i, distance in enumerate(distances):

        @pl.when(place[0] + distance < SIDE)
        def _(i=i, distance=distance):
            query = queries[distance - 1]
            before = None
            for link in queries[: distance - 1][::-1]:
                step = link[pl.ds(rows, C), :]
                before = step if before is None else left(nn(before, stacked(step)))
            for d in range(SIDE):
                move = suffixes[d]
                along[d] = move if before is None else left(nn(before, stacked(move)))
            for d in range(SIDE):
                for b in range(rows // ROWS):
                    here = pl.ds(b * ROWS, ROWS)
                    q = left(nn(query[here, :], stacked(along[d])))
                    state = None if d == 0 else (mx[here, :], ls[here, :], acc[here, :])
                    mx[here, :], ls[here, :], acc[here, :] = meet(q, *shards[d], state)
            outs[i][pl.ds(0, rows), :] = (acc[...] / ls[...]).astype(BF16)
            lines = []
            for n in range(rows // C):
                here = pl.ds(n * C, C)
                lse = mx[here, :] + jnp.log2(ls[here, :])
                lines.append(jnp.sum(jnp.where(row == col, lse, 0.0), axis=0, keepdims=True))
            lse = jnp.concatenate(lines, axis=0)
            high = lse.astype(BF16).astype(F32)
            middle = (lse - high).astype(BF16).astype(F32)
            low = lse - high - middle
            outs[i][pl.ds(rows, LSE_ROWS), :] = jnp.concatenate(
                [high, middle, low, jnp.zeros_like(lse)], axis=0
            ).astype(BF16)


def visitors(place, queries, suffixes, shards, distances):
    rows = queries[0].shape[0] - C
    count = len(distances)

    def kernel(*refs):
        visitors_kernel(*refs, distances=distances)

    return pl.pallas_call(
        kernel,
        out_shape=(jax.ShapeDtypeStruct((rows + LSE_ROWS, C), BF16),) * count,
        in_specs=[SCALARS] + [WHOLE] * (5 + SIDE),
        out_specs=(WHOLE,) * count,
        scratch_shapes=[pltpu.VMEM((rows, C), F32)] * 3 + [pltpu.VMEM((SIDE, C, 2 * C), BF16)],
        compiler_params=pltpu.CompilerParams(vmem_limit_bytes=VMEM_LIMIT),
        cost_estimate=cost(COST_VISIT * count),
        name="visitors",
    )(place, *queries, suffixes, *shards)


def merge_kernel(place, mx, ls, acc, r1, r2, r3, whole, *parts):
    rows = mx.shape[0]
    blocks = rows // C
    lines = []
    for d, r in enumerate((r1, r2, r3)):
        tail = r[pl.ds(rows, LSE_ROWS), :].astype(F32)
        lse = tail[0:blocks] + tail[blocks : 2 * blocks] + tail[2 * blocks : 3 * blocks]
        lines.append(jnp.where(place[0] > d, lse, NEGATIVE))
    for n in range(blocks):
        here = pl.ds(n * C, C)
        lse = [jnp.transpose(jnp.broadcast_to(line[n : n + 1, :], (C, C))) for line in lines]
        top = mx[here, :]
        for one in lse:
            top = jnp.maximum(top, one)
        share = jnp.exp2(mx[here, :] - top)
        total = ls[here, :] * share
        summed = acc[here, :] * share
        for d, r in enumerate((r1, r2, r3)):
            share = jnp.exp2(lse[d] - top)
            total += share
            summed += jnp.where(place[0] > d, share * r[here, :].astype(F32), 0.0)
        done = (summed / total).astype(BF16)
        whole[here, :] = done
        each = blocks // len(parts)
        parts[n // each][pl.ds((n % each) * C, C), :] = done


def merge(place, mx, ls, acc, returned, parts):
    rows = mx.shape[0]
    part = jax.ShapeDtypeStruct((rows // parts, C), BF16)
    return pl.pallas_call(
        merge_kernel,
        out_shape=(jax.ShapeDtypeStruct((rows, C), BF16),) + (part,) * parts,
        in_specs=[SCALARS] + [WHOLE] * 6,
        out_specs=(WHOLE,) * (1 + parts),
        compiler_params=pltpu.CompilerParams(vmem_limit_bytes=VMEM_LIMIT),
        cost_estimate=cost(2),
        name="merge",
    )(place, mx, ls, acc, *returned)


def project_kernel(place, here, there, columns, *rest):
    out = rest[-1]
    z, core = place[2], place[3]
    weights = []
    for s in range(SIDE):
        chip = lax.rem(z + (SIDE - s), SIDE)
        for head in (2 * chip + core, 2 * chip + 1 - core):
            weights.append(columns[pl.ds(pl.multiple_of(head * C, C), C), :])
    x = jnp.concatenate([p for s in range(SIDE) for p in (here[s], there[s])], axis=1)
    w = jnp.concatenate(weights, axis=0)
    out[...] = jnp.dot(x, w, preferred_element_type=F32).astype(BF16)


def project(place, here, there, columns, part, parts, so_far):
    rows = here.shape[1]
    width = columns.shape[1]
    extra = [] if so_far is None else [so_far]
    return pl.pallas_call(
        project_kernel,
        out_shape=jax.ShapeDtypeStruct((rows * parts, width), BF16),
        grid=(1,),
        in_specs=[SCALARS, WHOLE, WHOLE, WHOLE] + [ANY] * len(extra),
        out_specs=pl.BlockSpec((rows, width), lambda i: (part, 0)),
        input_output_aliases={4: 0} if extra else {},
        compiler_params=pltpu.CompilerParams(vmem_limit_bytes=VMEM_LIMIT),
        cost_estimate=cost(2),
        name="project",
    )(place, here, there, columns, *extra)


def deal_kernel(weight, out):
    width = out.shape[2]
    for n in range(out.shape[0]):
        out[n] = weight[:, pl.ds(n * width, width)]


def deal(weight):
    depth, width = weight.shape
    pieces = 2 * SIDE
    each = 2
    return pl.pallas_call(
        deal_kernel,
        out_shape=jax.ShapeDtypeStruct((pieces, depth, width // pieces), weight.dtype),
        grid=(pieces // each,),
        in_specs=[pl.BlockSpec((depth, each * width // pieces), lambda n: (0, n))],
        out_specs=pl.BlockSpec((each, depth, width // pieces), lambda n: (n, 0, 0)),
        compiler_params=pltpu.CompilerParams(vmem_limit_bytes=VMEM_LIMIT),
        cost_estimate=cost(COST_DEAL),
        name="deal",
    )(weight)


def along_y(x, d):
    return lax.ppermute(x, "ctx", [(i, i - i % SIDE + (i + d) % SIDE) for i in range(SIDE * SIDE)])


def down_x(x, d):
    return lax.ppermute(x, "ctx", [(i, i - SIDE * d) for i in range(SIDE * d, SIDE * SIDE)])


def up_x(x, d):
    return lax.ppermute(x, "ctx", [(i, i + SIDE * d) for i in range(SIDE * SIDE - SIDE * d)])


def along_z(x, d):
    return lax.ppermute(x, "head", [(i, (i + 2 * d) % (2 * SIDE)) for i in range(2 * SIDE)])


def other_core(x):
    return lax.ppermute(x, "head", [(i, i ^ 1) for i in range(2 * SIDE)])


PARTS = 2


def body(queries, keys, values, house, rates, out_weight):
    rows = queries.shape[0]
    blocks = rows // C
    number = lax.axis_index("ctx")
    head = lax.axis_index("head")
    place = jnp.stack([number // SIDE, number % SIDE, head // 2, head % 2]).astype(jnp.int32)
    q, k, v, h = (x[:, 0, :] for x in (queries, keys, values, house))
    step, sent, passages, prefixes, applied, rights, finals, unit = transport(k, v, h, rates.reshape(blocks, C))
    steps = [step] + [along_y(step, d) for d in (1, 2, 3)]
    leaving, suffixes, seens, starts = lead(place, q, prefixes, applied, unit, steps)
    visiting = [down_x(leaving, d) for d in (1, 2, 3)]
    before, after = along_y(sent, 1), along_y(sent, 3)
    moved, peak, total, summed = own(q, k, v, seens, starts, passages, rights, finals)
    held, moved = lax.optimization_barrier((out_weight, moved))
    dealt = deal(held)
    before, after, dealt = lax.optimization_barrier((before, after, dealt))
    columns = lax.all_to_all(dealt, "head", split_axis=0, concat_axis=0, tiled=True)
    columns = columns.reshape(2 * SIDE * C, columns.shape[2])
    shards = [sent, before, along_y(before[:rows], 1), along_y(after[rows:], 3), after]
    (two,) = visitors(place, visiting, suffixes, shards, (2,))
    sooner = up_x(two, 2)
    visiting[0], two = lax.optimization_barrier((visiting[0], two))
    one, three = visitors(place, visiting, suffixes, shards, (1, 3))
    returned = [up_x(one, 1), sooner, up_x(three, 3)]
    mx, ls, acc = row(place, moved, peak, total, summed, steps, shards)
    attended, *mine = merge(place, mx, ls, acc, returned, PARTS)
    pieces = []
    for x in mine:
        here = jnp.stack([x] + [along_z(x, d) for d in (1, 2, 3)])
        pieces.append((here, other_core(here)))
    projected = None
    for part, (here, there) in enumerate(pieces):
        projected = project(place, here, there, columns, part, PARTS, projected)
    return (attended[:, None, :], projected)


def solution(mesh):
    in_specs = (
        P("ctx", "head", None),
        P("ctx", "head", None),
        P("ctx", "head", None),
        P("ctx", "head", None),
        P("head", "ctx"),
        P("head", None),
    )
    out_specs = (P("ctx", "head", None), P("ctx", "head"))
    return jax.shard_map(body, mesh=mesh, in_specs=in_specs, out_specs=out_specs, check_vma=False)
```

```python
import jax
import jax.numpy as jnp
from jax import lax
from jax.experimental import pallas as pl
from jax.experimental.pallas import tpu as pltpu
from jax.sharding import PartitionSpec as P

C = 128
F32 = jnp.float32
BF16 = jnp.bfloat16
EPSILON = 1e-06
NEGATIVE = -1e30
LOG2E = 1.4426950408889634
VMEM_LIMIT = 56 * 1024 * 1024


def cost(microseconds):
    return pl.CostEstimate(flops=int(microseconds * 1.15e9), transcendentals=0, bytes_accessed=2**20)


def stacked(pair):
    return jnp.concatenate([pair, pair], axis=0)


def split(x):
    high = x.astype(BF16)
    return high, (x - high.astype(F32)).astype(BF16)


def left(x):
    return jnp.concatenate(split(x), axis=1)


def right_nn(x):
    pair = jnp.concatenate(split(x), axis=1)
    return jnp.concatenate([pair, pair], axis=0)


def right_nt(x):
    high, low = split(x)
    return jnp.concatenate(
        [jnp.concatenate([high, high], axis=1), jnp.concatenate([low, low], axis=1)], axis=0
    )


def halves(x):
    return x[:, : x.shape[1] // 2] + x[:, x.shape[1] // 2 :]


def nn(a, b):
    return halves(jnp.dot(a, b, preferred_element_type=F32))


def contract_last(a, b):
    return lax.dot_general(a, b, (((1,), (1,)), ((), ())), preferred_element_type=F32)


def nt(a, b):
    return halves(contract_last(a, b))


def unit_house(house):
    raw = house.astype(F32)
    return raw / jnp.sqrt(jnp.sum(raw * raw, axis=1, keepdims=True) + EPSILON)


def transport_kernel(keys, values, house, rates, step, sent, passages, prefixes, applied, rights, finals, unit):
    rows = keys.shape[0]
    sent[pl.ds(rows, rows), :] = values[...]
    blocks = rates.shape[0]
    row = lax.broadcasted_iota(jnp.int32, (C, C), 0)
    col = lax.broadcasted_iota(jnp.int32, (C, C), 1)
    eye = jnp.where(row == col, 1.0, 0.0).astype(F32)
    every = range(blocks)
    w = [unit_house(house[pl.ds(n * C, C), :]) for n in every]
    for n in every:
        unit[pl.ds(n * C, C), :] = w[n]
    wl = [left(x) for x in w]
    strict = []
    for n in every:
        gram = nt(wl[n], right_nt(w[n]))
        decay = jnp.transpose(jnp.broadcast_to(rates[n : n + 1, :], (C, C)))
        strict.append(jnp.where(row > col, gram, 0.0) * decay)
    x = [eye - jnp.where((row // 2) == (col // 2), strict[n], 0.0) for n in every]
    size = 2
    while size < C:
        band = ((row // (2 * size)) == (col // (2 * size))) & ((row // size) != (col // size))
        inner = [nn(left(jnp.where(band, strict[n], 0.0)), right_nn(x[n])) for n in every]
        x = [x[n] - nn(left(x[n]), right_nn(inner[n])) for n in every]
        size *= 2
    t = [x[n] * rates[n : n + 1, :] for n in every]
    final = []
    for n in every:
        k = keys[pl.ds(n * C, C), :]
        met = jnp.where(col > row, contract_last(jnp.concatenate([k, k], axis=1), wl[n]), 0.0)
        r = nt(left(met), right_nt(t[n]))
        rights[n] = r
        f = k.astype(F32) - nn(left(r), right_nn(w[n]))
        finals[pl.ds(n * C, C), :] = f
        final.append(f)
    passage = []
    for n in every:
        u = nn(left(t[n]), right_nn(w[n]))
        applied[n] = u
        passage.append(eye - nn(left(jnp.transpose(w[n])), right_nn(u)))
        passages[n] = passage[n]
    sent[pl.ds((blocks - 1) * C, C), :] = final[blocks - 1].astype(BF16)
    s = passage[blocks - 1]
    a = passage[0]
    prefixes[0] = left(eye)
    for n in range(blocks - 2, -1, -1):
        prefixes[blocks - 1 - n] = left(a)
        if n:
            a = nn(left(passage[blocks - 1 - n]), right_nn(a))
        sent[pl.ds(n * C, C), :] = nt(left(final[n]), right_nt(s)).astype(BF16)
        s = nn(left(s), right_nn(passage[n]))
    step[...] = left(s)


def transport(keys, values, house, rates):
    rows = keys.shape[0]
    blocks = rows // C
    square = jax.ShapeDtypeStruct((blocks, C, C), F32)
    flat = jax.ShapeDtypeStruct((rows, C), F32)
    return pl.pallas_call(
        transport_kernel,
        out_shape=(
            jax.ShapeDtypeStruct((C, 2 * C), BF16),
            jax.ShapeDtypeStruct((2 * rows, C), BF16),
            square,
            jax.ShapeDtypeStruct((blocks, C, 2 * C), BF16),
            square,
            square,
            flat,
            flat,
        ),
        cost_estimate=cost(8),
        compiler_params=pltpu.CompilerParams(vmem_limit_bytes=VMEM_LIMIT),
        name="transport",
    )(keys, values, house, rates)


SIDE = 4
COST_LEAD = 3
COST_OWN = 2
COST_VISIT = 3
COST_ROW = 6
COST_PAIR = 8


def lead_kernel(place, queries, prefixes, applied, unit, t0, t1, t2, t3, leaving, whole, suffixes, seens, starts, along, steps):
    blocks = applied.shape[0]
    rows = queries.shape[0]
    y = place[1]
    row = lax.broadcasted_iota(jnp.int32, (C, C), 0)
    col = lax.broadcasted_iota(jnp.int32, (C, C), 1)
    eye = jnp.where(row == col, 1.0, 0.0).astype(F32)
    along[...] = left(eye)
    for d, t in enumerate((t0, t1, t2, t3)):
        steps[lax.rem(y + (SIDE - d), SIDE)] = t[...]
        if d:

            @pl.when(y >= d)
            def _(t=t):
                along[...] = left(nn(along[...], stacked(t[...])))

    suffix = left(eye)
    for n in range(SIDE - 1, -1, -1):
        suffixes[lax.rem(y + (SIDE - n), SIDE)] = suffix
        suffix = left(nn(suffix, stacked(steps[n])))
    move = stacked(along[...])
    for n in range(blocks):
        here = pl.ds(n * C, C)
        q = queries[here, :].astype(F32) * (C**-0.5 * LOG2E)
        seen = left(jnp.where(row >= col, nt(left(q), right_nt(unit[here, :])), 0.0))
        start = left(q - nn(seen, right_nn(applied[n])))
        seens[here, :] = seen
        starts[here, :] = start
        out = left(nn(start, stacked(left(nn(prefixes[n], move)))))
        leaving[here, :] = out
    leaving[pl.ds(rows, C), :] = suffix
    whole[...] = suffix


def lead(place, queries, prefixes, applied, unit, steps):
    rows = queries.shape[0]
    pair = jax.ShapeDtypeStruct((rows, 2 * C), BF16)
    return pl.pallas_call(
        lead_kernel,
        out_shape=(
            jax.ShapeDtypeStruct((rows + C, 2 * C), BF16),
            jax.ShapeDtypeStruct((C, 2 * C), BF16),
            jax.ShapeDtypeStruct((SIDE, C, 2 * C), BF16),
            pair,
            pair,
        ),
        in_specs=[SCALARS] + [WHOLE] * (4 + SIDE),
        out_specs=(WHOLE,) * 5,
        scratch_shapes=[pltpu.VMEM((C, 2 * C), BF16), pltpu.VMEM((SIDE, C, 2 * C), BF16)],
        compiler_params=pltpu.CompilerParams(vmem_limit_bytes=VMEM_LIMIT),
        cost_estimate=cost(COST_LEAD),
        name="lead",
    )(place, queries, prefixes, applied, unit, *steps)


def own_kernel(
    queries, keys, values, seens, starts, passages, rights, finals, weight,
    moved, peak, total, summed, dealt, table, hand, sems
):
    blocks = passages.shape[0]
    pieces, _, width = dealt.shape
    taken = [
        pltpu.make_async_copy(weight.at[:, pl.ds(n * width, width)], hand.at[n], sems.at[0, n]) for n in range(pieces)
    ]
    given = [pltpu.make_async_copy(hand.at[n], dealt.at[n], sems.at[1, n]) for n in range(pieces)]
    for copy in taken:
        copy.start()
    row = lax.broadcasted_iota(jnp.int32, (C, C), 0)
    col = lax.broadcasted_iota(jnp.int32, (C, C), 1)
    for n in range(blocks):
        here = pl.ds(n * C, C)
        q = queries[here, :].astype(F32) * (C**-0.5 * LOG2E)
        k = keys[here, :]
        inside = contract_last(left(q), jnp.concatenate([k, k], axis=1)) - nt(seens[here, :], right_nt(rights[n]))
        table[here, here] = jnp.where(row >= col, inside, NEGATIVE)
        moved[here, :] = starts[here, :]
    for m in range(blocks - 2, -1, -1):
        here = pl.ds(m * C, C)
        after = pl.ds((m + 1) * C, (blocks - 1 - m) * C)
        block_rows = moved[after, :]
        table[after, here] = nt(block_rows, right_nt(finals[here, :]))
        moved[after, :] = left(nn(block_rows, right_nn(passages[m])))
    for n in range(pieces):
        taken[n].wait()
        given[n].start()
    for n in range(blocks):
        here = pl.ds(n * C, C)
        upto = pl.ds(0, (n + 1) * C)
        s = table[here, upto]
        m = jnp.max(s, axis=1, keepdims=True)
        p = jnp.exp2(s - m)
        peak[here, :] = jnp.broadcast_to(m, (C, C))
        total[here, :] = jnp.broadcast_to(jnp.sum(p, axis=1, keepdims=True), (C, C))
        summed[here, :] = jnp.dot(p.astype(BF16), values[upto, :], preferred_element_type=F32)
    for copy in given:
        copy.wait()


def own(queries, keys, values, seens, starts, passages, rights, finals, weight):
    rows = values.shape[0]
    pieces = 2 * SIDE
    dealt = (pieces, weight.shape[0], weight.shape[1] // pieces)
    flat = jax.ShapeDtypeStruct((rows, C), F32)
    return pl.pallas_call(
        own_kernel,
        out_shape=(
            jax.ShapeDtypeStruct((rows, 2 * C), BF16),
            flat,
            flat,
            flat,
            jax.ShapeDtypeStruct(dealt, weight.dtype),
        ),
        in_specs=[WHOLE] * 8 + [ANY],
        out_specs=(WHOLE,) * 4 + (ANY,),
        scratch_shapes=[
            pltpu.VMEM((rows, rows), F32),
            pltpu.VMEM(dealt, weight.dtype),
            pltpu.SemaphoreType.DMA((2, pieces)),
        ],
        compiler_params=pltpu.CompilerParams(vmem_limit_bytes=VMEM_LIMIT),
        cost_estimate=cost(COST_OWN),
        name="own",
    )(queries, keys, values, seens, starts, passages, rights, finals, weight)


ROWS = 512
LSE_ROWS = 32
ANY = pl.BlockSpec(memory_space=pl.ANY)
SCALARS = pl.BlockSpec(memory_space=pltpu.SMEM)
WHOLE = pl.BlockSpec(memory_space=pltpu.VMEM)


def meet(q, keys, values, state):
    rows = keys.shape[0]
    k = keys[...]
    v = values[...]
    s = contract_last(q, jnp.concatenate([k, k], axis=1))
    top = jnp.max(s, axis=1, keepdims=True)
    if state is None:
        new = jnp.broadcast_to(top, (q.shape[0], C))
    else:
        new = jnp.maximum(state[0], top)
    p = jnp.exp2(s - jnp.tile(new, (1, rows // C))).astype(BF16)
    pv = jnp.dot(p, jnp.concatenate([v, jnp.ones_like(v)], axis=1), preferred_element_type=F32)
    if state is None:
        return new, pv[:, C:], pv[:, :C]
    shrink = jnp.exp2(state[0] - new)
    return new, state[1] * shrink + pv[:, C:], state[2] * shrink + pv[:, :C]


def row_kernel(place, moved, peak, total, summed, t1, t2, s1, k2, v2, s3, mx, ls, acc, mv):
    y = place[1]
    rows = moved.shape[0]
    mv[...] = moved[...]
    mx[...] = peak[...]
    ls[...] = total[...]
    acc[...] = summed[...]
    halves_of = lambda s: (s.at[pl.ds(0, rows)], s.at[pl.ds(rows, rows)])
    for d, (t, shard) in enumerate(((t1, halves_of(s1)), (t2, (k2, v2)), (None, halves_of(s3)))):

        @pl.when(y > d)
        def _(t=t, shard=shard):
            for b in range(rows // ROWS):
                here = pl.ds(b * ROWS, ROWS)
                q = mv[here, :]
                mx[here, :], ls[here, :], acc[here, :] = meet(
                    q, *shard, (mx[here, :], ls[here, :], acc[here, :])
                )
                if t is not None:
                    mv[here, :] = left(nn(q, stacked(t[...])))


def row(place, moved, peak, total, summed, steps, shards):
    rows = moved.shape[0]
    flat = jax.ShapeDtypeStruct((rows, C), F32)
    return pl.pallas_call(
        row_kernel,
        out_shape=(flat, flat, flat),
        in_specs=[SCALARS] + [WHOLE] * 10,
        out_specs=(WHOLE, WHOLE, WHOLE),
        scratch_shapes=[pltpu.VMEM((rows, 2 * C), BF16)],
        compiler_params=pltpu.CompilerParams(vmem_limit_bytes=VMEM_LIMIT),
        cost_estimate=cost(COST_ROW),
        name="row",
    )(place, moved, peak, total, summed, steps[1], steps[2], *shards[1:])


def visitors_kernel(place, suffixes, s0, s1, k2, v2, s3, *rest, hops):
    mx, ls, acc, along = rest[-4:]
    outs = rest[-4 - len(hops) : -4]
    rows = mx.shape[0]
    shards = [(s.at[pl.ds(0, rows)], s.at[pl.ds(rows, rows)]) for s in (s0, s1, s3)]
    shards.insert(2, (k2, v2))
    row = lax.broadcasted_iota(jnp.int32, (C, C), 0)
    col = lax.broadcasted_iota(jnp.int32, (C, C), 1)
    at = 0
    for out, count in zip(outs, hops):
        query, links = rest[at], rest[at + 1 : at + 1 + count]
        at += 1 + count

        @pl.when(place[0] + count + 1 < SIDE)
        def _(out=out, query=query, links=links):
            before = None
            for link in links[::-1]:
                before = link[...] if before is None else left(nn(before, stacked(link[...])))
            for d in range(SIDE):
                move = suffixes[d]
                along[d] = move if before is None else left(nn(before, stacked(move)))
            for d in range(SIDE):
                for b in range(rows // ROWS):
                    here = pl.ds(b * ROWS, ROWS)
                    q = left(nn(query[here, :], stacked(along[d])))
                    state = None if d == 0 else (mx[here, :], ls[here, :], acc[here, :])
                    mx[here, :], ls[here, :], acc[here, :] = meet(q, *shards[d], state)
            out[pl.ds(0, rows), :] = (acc[...] / ls[...]).astype(BF16)
            lines = []
            for n in range(rows // C):
                here = pl.ds(n * C, C)
                lse = mx[here, :] + jnp.log2(ls[here, :])
                lines.append(jnp.sum(jnp.where(row == col, lse, 0.0), axis=0, keepdims=True))
            lse = jnp.concatenate(lines, axis=0)
            high = lse.astype(BF16).astype(F32)
            middle = (lse - high).astype(BF16).astype(F32)
            low = lse - high - middle
            out[pl.ds(rows, LSE_ROWS), :] = jnp.concatenate(
                [high, middle, low, jnp.zeros_like(lse)], axis=0
            ).astype(BF16)


def visitors(place, suffixes, shards, jobs):
    rows = jobs[0][0].shape[0] - C
    count = len(jobs)
    hops = tuple(len(links) for _, links in jobs)
    specs = []
    given = []
    for query, links in jobs:
        specs.append(pl.BlockSpec((rows, 2 * C), lambda i: (0, 0)))
        specs += [pl.BlockSpec((C, 2 * C), lambda i, n=link.shape[0] // C - 1: (n, 0)) for link in links]
        given += [query, *links]

    def kernel(*refs):
        visitors_kernel(*refs, hops=hops)

    return pl.pallas_call(
        kernel,
        out_shape=(jax.ShapeDtypeStruct((rows + LSE_ROWS, C), BF16),) * count,
        grid=(1,),
        in_specs=[SCALARS] + [WHOLE] * (2 + SIDE) + specs,
        out_specs=(WHOLE,) * count,
        scratch_shapes=[pltpu.VMEM((rows, C), F32)] * 3 + [pltpu.VMEM((SIDE, C, 2 * C), BF16)],
        compiler_params=pltpu.CompilerParams(vmem_limit_bytes=VMEM_LIMIT),
        cost_estimate=cost(COST_VISIT if count == 1 else COST_PAIR),
        name="visitors",
    )(place, suffixes, *shards, *given)


def merge_kernel(place, mx, ls, acc, r1, r2, r3, whole):
    rows = mx.shape[0]
    blocks = rows // C
    lines = []
    for d, r in enumerate((r1, r2, r3)):
        tail = r[pl.ds(rows, LSE_ROWS), :].astype(F32)
        lse = tail[0:blocks] + tail[blocks : 2 * blocks] + tail[2 * blocks : 3 * blocks]
        lines.append(jnp.where(place[0] > d, lse, NEGATIVE))
    for n in range(blocks):
        here = pl.ds(n * C, C)
        lse = [jnp.transpose(jnp.broadcast_to(line[n : n + 1, :], (C, C))) for line in lines]
        top = mx[here, :]
        for one in lse:
            top = jnp.maximum(top, one)
        share = jnp.exp2(mx[here, :] - top)
        total = ls[here, :] * share
        summed = acc[here, :] * share
        for d, r in enumerate((r1, r2, r3)):
            share = jnp.exp2(lse[d] - top)
            total += share
            summed += jnp.where(place[0] > d, share * r[here, :].astype(F32), 0.0)
        whole[here, :] = (summed / total).astype(BF16)


def merge(place, mx, ls, acc, returned):
    rows = mx.shape[0]
    return pl.pallas_call(
        merge_kernel,
        out_shape=jax.ShapeDtypeStruct((rows, C), BF16),
        in_specs=[SCALARS] + [WHOLE] * 6,
        out_specs=WHOLE,
        compiler_params=pltpu.CompilerParams(vmem_limit_bytes=VMEM_LIMIT),
        cost_estimate=cost(2),
        name="merge",
    )(place, mx, ls, acc, *returned)


def along_y(x, d):
    return lax.ppermute(x, "ctx", [(i, i - i % SIDE + (i + d) % SIDE) for i in range(SIDE * SIDE)])


def down_x(x, d):
    return lax.ppermute(x, "ctx", [(i, i - SIDE * d) for i in range(SIDE * d, SIDE * SIDE)])


def up_x(x, d):
    return lax.ppermute(x, "ctx", [(i, i + SIDE * d) for i in range(SIDE * SIDE - SIDE * d)])


def along_z(x, d):
    return lax.ppermute(x, "head", [(i, (i + 2 * d) % (2 * SIDE)) for i in range(2 * SIDE)])


def other_core(x):
    return lax.ppermute(x, "head", [(i, i ^ 1) for i in range(2 * SIDE)])


def body(queries, keys, values, house, rates, out_weight):
    rows = queries.shape[0]
    blocks = rows // C
    number = lax.axis_index("ctx")
    head = lax.axis_index("head")
    place = jnp.stack([number // SIDE, number % SIDE, head // 2, head % 2]).astype(jnp.int32)
    q, k, v, h = (x[:, 0, :] for x in (queries, keys, values, house))
    step, sent, passages, prefixes, applied, rights, finals, unit = transport(k, v, h, rates.reshape(blocks, C))
    steps = [step] + [along_y(step, d) for d in (1, 2, 3)]
    leaving, whole, suffixes, seens, starts = lead(place, q, prefixes, applied, unit, steps)
    first, third, second_link = down_x(leaving, 1), down_x(leaving, 3), down_x(whole, 2)
    before, after = along_y(sent, 1), along_y(sent, 3)
    moved, peak, total, summed, dealt = own(q, k, v, seens, starts, passages, rights, finals, out_weight)
    before, after, dealt = lax.optimization_barrier((before, after, dealt))
    columns = lax.all_to_all(dealt, "head", split_axis=0, concat_axis=0, tiled=True)
    shards = [sent, before, along_y(before[:rows], 1), along_y(after[rows:], 3), after]
    relayed, moved = lax.optimization_barrier((first, moved))
    second = down_x(relayed, 1)
    one, three = visitors(place, suffixes, shards, [(first, []), (third, [first, second_link])])
    second, one = lax.optimization_barrier((second, one))
    (two,) = visitors(place, suffixes, shards, [(second, [first])])
    returned = [up_x(one, 1), up_x(two, 2), up_x(three, 3)]
    mx, ls, acc = row(place, moved, peak, total, summed, steps, shards)
    attended = merge(place, mx, ls, acc, returned)
    half = rows // 2
    left_chip, right_chip = along_z(attended, 1), along_z(attended, 3)
    three_chips = jnp.stack([attended, left_chip, right_chip])
    upper, lower = along_z(left_chip[:half], 1), along_z(right_chip[half:], 3)

    def weights(core, offsets):
        return jnp.stack(
            [lax.dynamic_index_in_dim(columns, 2 * ((place[2] + d) % SIDE) + core, 0, False) for d in offsets]
        )

    def part(x, core, offsets):
        return jnp.einsum("srk,skn->rn", x, weights(core, offsets), preferred_element_type=F32)

    mine, theirs = place[3], 1 - place[3]
    projected = part(three_chips, mine, (0, SIDE - 1, 1))
    upper, lower, projected = lax.optimization_barrier((upper, lower, projected))
    across = jnp.concatenate([upper, lower], axis=0)
    projected = projected + part(other_core(three_chips), theirs, (0, SIDE - 1, 1))
    projected = projected + part(across[None], mine, (2,))
    projected = projected + part(other_core(across)[None], theirs, (2,))
    return (attended[:, None, :], projected.astype(BF16))


def solution(mesh):
    in_specs = (
        P("ctx", "head", None),
        P("ctx", "head", None),
        P("ctx", "head", None),
        P("ctx", "head", None),
        P("head", "ctx"),
        P("head", None),
    )
    out_specs = (P("ctx", "head", None), P("ctx", "head"))
    return jax.shard_map(body, mesh=mesh, in_specs=in_specs, out_specs=out_specs, check_vma=False)
```

```python
import jax
import jax.numpy as jnp
from jax import lax
from jax.experimental import pallas as pl
from jax.experimental.pallas import tpu as pltpu
from jax.sharding import PartitionSpec as P

C = 128
F32 = jnp.float32
BF16 = jnp.bfloat16
EPSILON = 1e-06
NEGATIVE = -1e30
LOG2E = 1.4426950408889634
VMEM_LIMIT = 56 * 1024 * 1024


def cost(microseconds):
    return pl.CostEstimate(flops=int(microseconds * 1.15e9), transcendentals=0, bytes_accessed=2**20)


def stacked(pair):
    return jnp.concatenate([pair, pair], axis=0)


def split(x):
    high = x.astype(BF16)
    return high, (x - high.astype(F32)).astype(BF16)


def left(x):
    return jnp.concatenate(split(x), axis=1)


def right_nn(x):
    pair = jnp.concatenate(split(x), axis=1)
    return jnp.concatenate([pair, pair], axis=0)


def right_nt(x):
    high, low = split(x)
    return jnp.concatenate(
        [jnp.concatenate([high, high], axis=1), jnp.concatenate([low, low], axis=1)], axis=0
    )


def halves(x):
    return x[:, : x.shape[1] // 2] + x[:, x.shape[1] // 2 :]


def nn(a, b):
    return halves(jnp.dot(a, b, preferred_element_type=F32))


def contract_last(a, b):
    return lax.dot_general(a, b, (((1,), (1,)), ((), ())), preferred_element_type=F32)


def nt(a, b):
    return halves(contract_last(a, b))


def unit_house(house):
    raw = house.astype(F32)
    return raw / jnp.sqrt(jnp.sum(raw * raw, axis=1, keepdims=True) + EPSILON)


def transport_kernel(keys, values, house, rates, step, sent, passages, prefixes, applied, rights, finals, unit):
    rows = keys.shape[0]
    sent[pl.ds(rows, rows), :] = values[...]
    blocks = rates.shape[0]
    row = lax.broadcasted_iota(jnp.int32, (C, C), 0)
    col = lax.broadcasted_iota(jnp.int32, (C, C), 1)
    eye = jnp.where(row == col, 1.0, 0.0).astype(F32)
    every = range(blocks)
    w = [unit_house(house[pl.ds(n * C, C), :]) for n in every]
    for n in every:
        unit[pl.ds(n * C, C), :] = w[n]
    wl = [left(x) for x in w]
    strict = []
    for n in every:
        gram = nt(wl[n], right_nt(w[n]))
        decay = jnp.transpose(jnp.broadcast_to(rates[n : n + 1, :], (C, C)))
        strict.append(jnp.where(row > col, gram, 0.0) * decay)
    x = [eye - jnp.where((row // 2) == (col // 2), strict[n], 0.0) for n in every]
    size = 2
    while size < C:
        band = ((row // (2 * size)) == (col // (2 * size))) & ((row // size) != (col // size))
        inner = [nn(left(jnp.where(band, strict[n], 0.0)), right_nn(x[n])) for n in every]
        x = [x[n] - nn(left(x[n]), right_nn(inner[n])) for n in every]
        size *= 2
    t = [x[n] * rates[n : n + 1, :] for n in every]
    final = []
    for n in every:
        k = keys[pl.ds(n * C, C), :]
        met = jnp.where(col > row, contract_last(jnp.concatenate([k, k], axis=1), wl[n]), 0.0)
        r = nt(left(met), right_nt(t[n]))
        rights[n] = r
        f = k.astype(F32) - nn(left(r), right_nn(w[n]))
        finals[pl.ds(n * C, C), :] = f
        final.append(f)
    passage = []
    for n in every:
        u = nn(left(t[n]), right_nn(w[n]))
        applied[n] = u
        passage.append(eye - nn(left(jnp.transpose(w[n])), right_nn(u)))
        passages[n] = passage[n]
    sent[pl.ds((blocks - 1) * C, C), :] = final[blocks - 1].astype(BF16)
    s = passage[blocks - 1]
    a = passage[0]
    prefixes[0] = left(eye)
    for n in range(blocks - 2, -1, -1):
        prefixes[blocks - 1 - n] = left(a)
        if n:
            a = nn(left(passage[blocks - 1 - n]), right_nn(a))
        sent[pl.ds(n * C, C), :] = nt(left(final[n]), right_nt(s)).astype(BF16)
        s = nn(left(s), right_nn(passage[n]))
    step[...] = left(s)


def transport(keys, values, house, rates):
    rows = keys.shape[0]
    blocks = rows // C
    square = jax.ShapeDtypeStruct((blocks, C, C), F32)
    flat = jax.ShapeDtypeStruct((rows, C), F32)
    return pl.pallas_call(
        transport_kernel,
        out_shape=(
            jax.ShapeDtypeStruct((C, 2 * C), BF16),
            jax.ShapeDtypeStruct((2 * rows, C), BF16),
            square,
            jax.ShapeDtypeStruct((blocks, C, 2 * C), BF16),
            square,
            square,
            flat,
            flat,
        ),
        cost_estimate=cost(8),
        compiler_params=pltpu.CompilerParams(vmem_limit_bytes=VMEM_LIMIT),
        name="transport",
    )(keys, values, house, rates)


SIDE = 4
COST_LEAD = 3
COST_OWN = 2
COST_VISIT = 3
COST_ROW = 6
COST_PAIR = 8


def lead_kernel(place, queries, prefixes, applied, unit, t0, t1, t2, t3, leaving, whole, suffixes, seens, starts, along, steps):
    blocks = applied.shape[0]
    rows = queries.shape[0]
    y = place[1]
    row = lax.broadcasted_iota(jnp.int32, (C, C), 0)
    col = lax.broadcasted_iota(jnp.int32, (C, C), 1)
    eye = jnp.where(row == col, 1.0, 0.0).astype(F32)
    along[...] = left(eye)
    for d, t in enumerate((t0, t1, t2, t3)):
        steps[lax.rem(y + (SIDE - d), SIDE)] = t[...]
        if d:

            @pl.when(y >= d)
            def _(t=t):
                along[...] = left(nn(along[...], stacked(t[...])))

    suffix = left(eye)
    for n in range(SIDE - 1, -1, -1):
        suffixes[lax.rem(y + (SIDE - n), SIDE)] = suffix
        suffix = left(nn(suffix, stacked(steps[n])))
    move = stacked(along[...])
    for n in range(blocks):
        here = pl.ds(n * C, C)
        q = queries[here, :].astype(F32) * (C**-0.5 * LOG2E)
        seen = left(jnp.where(row >= col, nt(left(q), right_nt(unit[here, :])), 0.0))
        start = left(q - nn(seen, right_nn(applied[n])))
        seens[here, :] = seen
        starts[here, :] = start
        out = left(nn(start, stacked(left(nn(prefixes[n], move)))))
        leaving[here, :] = out
    leaving[pl.ds(rows, C), :] = suffix
    whole[...] = suffix


def lead(place, queries, prefixes, applied, unit, steps):
    rows = queries.shape[0]
    pair = jax.ShapeDtypeStruct((rows, 2 * C), BF16)
    return pl.pallas_call(
        lead_kernel,
        out_shape=(
            jax.ShapeDtypeStruct((rows + C, 2 * C), BF16),
            jax.ShapeDtypeStruct((C, 2 * C), BF16),
            jax.ShapeDtypeStruct((SIDE, C, 2 * C), BF16),
            pair,
            pair,
        ),
        in_specs=[SCALARS] + [WHOLE] * (4 + SIDE),
        out_specs=(WHOLE,) * 5,
        scratch_shapes=[pltpu.VMEM((C, 2 * C), BF16), pltpu.VMEM((SIDE, C, 2 * C), BF16)],
        compiler_params=pltpu.CompilerParams(vmem_limit_bytes=VMEM_LIMIT),
        cost_estimate=cost(COST_LEAD),
        name="lead",
    )(place, queries, prefixes, applied, unit, *steps)


def own_kernel(
    queries, keys, values, seens, starts, passages, rights, finals, weight,
    moved, peak, total, summed, dealt, table, hand, sems
):
    blocks = passages.shape[0]
    pieces, _, width = dealt.shape
    taken = [
        pltpu.make_async_copy(weight.at[:, pl.ds(n * width, width)], hand.at[n], sems.at[0, n]) for n in range(pieces)
    ]
    given = [pltpu.make_async_copy(hand.at[n], dealt.at[n], sems.at[1, n]) for n in range(pieces)]
    for copy in taken:
        copy.start()
    row = lax.broadcasted_iota(jnp.int32, (C, C), 0)
    col = lax.broadcasted_iota(jnp.int32, (C, C), 1)
    for n in range(blocks):
        here = pl.ds(n * C, C)
        q = queries[here, :].astype(F32) * (C**-0.5 * LOG2E)
        k = keys[here, :]
        inside = contract_last(left(q), jnp.concatenate([k, k], axis=1)) - nt(seens[here, :], right_nt(rights[n]))
        table[here, here] = jnp.where(row >= col, inside, NEGATIVE)
        moved[here, :] = starts[here, :]
    for m in range(blocks - 2, -1, -1):
        here = pl.ds(m * C, C)
        after = pl.ds((m + 1) * C, (blocks - 1 - m) * C)
        block_rows = moved[after, :]
        table[after, here] = nt(block_rows, right_nt(finals[here, :]))
        moved[after, :] = left(nn(block_rows, right_nn(passages[m])))
    for n in range(pieces):
        taken[n].wait()
        given[n].start()
    for n in range(blocks):
        here = pl.ds(n * C, C)
        upto = pl.ds(0, (n + 1) * C)
        s = table[here, upto]
        m = jnp.max(s, axis=1, keepdims=True)
        p = jnp.exp2(s - m)
        peak[here, :] = jnp.broadcast_to(m, (C, C))
        total[here, :] = jnp.broadcast_to(jnp.sum(p, axis=1, keepdims=True), (C, C))
        summed[here, :] = jnp.dot(p.astype(BF16), values[upto, :], preferred_element_type=F32)
    for copy in given:
        copy.wait()


def own(queries, keys, values, seens, starts, passages, rights, finals, weight):
    rows = values.shape[0]
    pieces = 2 * SIDE
    dealt = (pieces, weight.shape[0], weight.shape[1] // pieces)
    flat = jax.ShapeDtypeStruct((rows, C), F32)
    return pl.pallas_call(
        own_kernel,
        out_shape=(
            jax.ShapeDtypeStruct((rows, 2 * C), BF16),
            flat,
            flat,
            flat,
            jax.ShapeDtypeStruct(dealt, weight.dtype),
        ),
        in_specs=[WHOLE] * 8 + [ANY],
        out_specs=(WHOLE,) * 4 + (ANY,),
        scratch_shapes=[
            pltpu.VMEM((rows, rows), F32),
            pltpu.VMEM(dealt, weight.dtype),
            pltpu.SemaphoreType.DMA((2, pieces)),
        ],
        compiler_params=pltpu.CompilerParams(vmem_limit_bytes=VMEM_LIMIT),
        cost_estimate=cost(COST_OWN),
        name="own",
    )(queries, keys, values, seens, starts, passages, rights, finals, weight)


ROWS = 512
LSE_ROWS = 32
ANY = pl.BlockSpec(memory_space=pl.ANY)
SCALARS = pl.BlockSpec(memory_space=pltpu.SMEM)
WHOLE = pl.BlockSpec(memory_space=pltpu.VMEM)


def meet(q, keys, values, state):
    rows = keys.shape[0]
    k = keys[...]
    v = values[...]
    s = contract_last(q, jnp.concatenate([k, k], axis=1))
    top = jnp.max(s, axis=1, keepdims=True)
    if state is None:
        new = jnp.broadcast_to(top, (q.shape[0], C))
    else:
        new = jnp.maximum(state[0], top)
    p = jnp.exp2(s - jnp.tile(new, (1, rows // C))).astype(BF16)
    pv = jnp.dot(p, jnp.concatenate([v, jnp.ones_like(v)], axis=1), preferred_element_type=F32)
    if state is None:
        return new, pv[:, C:], pv[:, :C]
    shrink = jnp.exp2(state[0] - new)
    return new, state[1] * shrink + pv[:, C:], state[2] * shrink + pv[:, :C]


def settle(out, mx, ls, acc):
    rows = mx.shape[0]
    row = lax.broadcasted_iota(jnp.int32, (C, C), 0)
    col = lax.broadcasted_iota(jnp.int32, (C, C), 1)
    out[pl.ds(0, rows), :] = (acc[...] / ls[...]).astype(BF16)
    lines = []
    for n in range(rows // C):
        here = pl.ds(n * C, C)
        lse = mx[here, :] + jnp.log2(ls[here, :])
        lines.append(jnp.sum(jnp.where(row == col, lse, 0.0), axis=0, keepdims=True))
    lse = jnp.concatenate(lines, axis=0)
    high = lse.astype(BF16).astype(F32)
    middle = (lse - high).astype(BF16).astype(F32)
    low = lse - high - middle
    out[pl.ds(rows, LSE_ROWS), :] = jnp.concatenate([high, middle, low, jnp.zeros_like(lse)], axis=0).astype(BF16)


def row_kernel(place, moved, t1, t2, s1, k2, v2, s3, out, mx, ls, acc, mv):
    y = place[1]
    rows = moved.shape[0]
    mv[...] = moved[...]
    parts = [(s.at[pl.ds(0, rows)], s.at[pl.ds(rows, rows)]) for s in (s1, s3)]
    parts.insert(1, (k2, v2))
    for d, (t, shard) in enumerate(zip((t1, t2, None), parts)):

        @pl.when(y > d)
        def _(d=d, t=t, shard=shard):
            for b in range(rows // ROWS):
                here = pl.ds(b * ROWS, ROWS)
                q = mv[here, :]
                state = (mx[here, :], ls[here, :], acc[here, :]) if d else None
                mx[here, :], ls[here, :], acc[here, :] = meet(q, *shard, state)
                if t is not None:
                    mv[here, :] = left(nn(q, stacked(t[...])))

    @pl.when(y > 0)
    def _():
        settle(out, mx, ls, acc)


def row(place, moved, steps, shards):
    rows = moved.shape[0]
    return pl.pallas_call(
        row_kernel,
        out_shape=jax.ShapeDtypeStruct((rows + LSE_ROWS, C), BF16),
        in_specs=[SCALARS] + [WHOLE] * 7,
        out_specs=WHOLE,
        scratch_shapes=[pltpu.VMEM((rows, C), F32)] * 3 + [pltpu.VMEM((rows, 2 * C), BF16)],
        compiler_params=pltpu.CompilerParams(vmem_limit_bytes=VMEM_LIMIT),
        cost_estimate=cost(COST_ROW),
        name="row",
    )(place, moved, steps[1], steps[2], *shards[1:])


def visitors_kernel(place, suffixes, s0, s1, k2, v2, s3, *rest, hops):
    mx, ls, acc, along = rest[-4:]
    outs = rest[-4 - len(hops) : -4]
    rows = mx.shape[0]
    shards = [(s.at[pl.ds(0, rows)], s.at[pl.ds(rows, rows)]) for s in (s0, s1, s3)]
    shards.insert(2, (k2, v2))
    at = 0
    for out, count in zip(outs, hops):
        query, links = rest[at], rest[at + 1 : at + 1 + count]
        at += 1 + count

        @pl.when(place[0] + count + 1 < SIDE)
        def _(out=out, query=query, links=links):
            before = None
            for link in links[::-1]:
                before = link[...] if before is None else left(nn(before, stacked(link[...])))
            for d in range(SIDE):
                move = suffixes[d]
                along[d] = move if before is None else left(nn(before, stacked(move)))
            for d in range(SIDE):
                for b in range(rows // ROWS):
                    here = pl.ds(b * ROWS, ROWS)
                    q = left(nn(query[here, :], stacked(along[d])))
                    state = None if d == 0 else (mx[here, :], ls[here, :], acc[here, :])
                    mx[here, :], ls[here, :], acc[here, :] = meet(q, *shards[d], state)
            settle(out, mx, ls, acc)


def visitors(place, suffixes, shards, jobs):
    rows = jobs[0][0].shape[0] - C
    count = len(jobs)
    hops = tuple(len(links) for _, links in jobs)
    specs = []
    given = []
    for query, links in jobs:
        specs.append(pl.BlockSpec((rows, 2 * C), lambda i: (0, 0)))
        specs += [pl.BlockSpec((C, 2 * C), lambda i, n=link.shape[0] // C - 1: (n, 0)) for link in links]
        given += [query, *links]

    def kernel(*refs):
        visitors_kernel(*refs, hops=hops)

    return pl.pallas_call(
        kernel,
        out_shape=(jax.ShapeDtypeStruct((rows + LSE_ROWS, C), BF16),) * count,
        grid=(1,),
        in_specs=[SCALARS] + [WHOLE] * (2 + SIDE) + specs,
        out_specs=(WHOLE,) * count,
        scratch_shapes=[pltpu.VMEM((rows, C), F32)] * 3 + [pltpu.VMEM((SIDE, C, 2 * C), BF16)],
        compiler_params=pltpu.CompilerParams(vmem_limit_bytes=VMEM_LIMIT),
        cost_estimate=cost(COST_VISIT if count == 1 else COST_PAIR),
        name="visitors",
    )(place, suffixes, *shards, *given)


def merge_kernel(place, mx, ls, acc, own_row, r1, r2, r3, whole):
    rows = mx.shape[0]
    blocks = rows // C
    partials = ((own_row, place[1] > 0), (r1, place[0] > 0), (r2, place[0] > 1), (r3, place[0] > 2))
    lines = []
    for r, there in partials:
        tail = r[pl.ds(rows, LSE_ROWS), :].astype(F32)
        lse = tail[0:blocks] + tail[blocks : 2 * blocks] + tail[2 * blocks : 3 * blocks]
        lines.append(jnp.where(there, lse, NEGATIVE))
    for n in range(blocks):
        here = pl.ds(n * C, C)
        lse = [jnp.transpose(jnp.broadcast_to(line[n : n + 1, :], (C, C))) for line in lines]
        top = mx[here, :]
        for one in lse:
            top = jnp.maximum(top, one)
        share = jnp.exp2(mx[here, :] - top)
        total = ls[here, :] * share
        summed = acc[here, :] * share
        for one, (r, there) in zip(lse, partials):
            share = jnp.exp2(one - top)
            total += share
            summed += jnp.where(there, share * r[here, :].astype(F32), 0.0)
        whole[here, :] = (summed / total).astype(BF16)


def merge(place, mx, ls, acc, partials):
    rows = mx.shape[0]
    return pl.pallas_call(
        merge_kernel,
        out_shape=jax.ShapeDtypeStruct((rows, C), BF16),
        in_specs=[SCALARS] + [WHOLE] * 7,
        out_specs=WHOLE,
        compiler_params=pltpu.CompilerParams(vmem_limit_bytes=VMEM_LIMIT),
        cost_estimate=cost(2),
        name="merge",
    )(place, mx, ls, acc, *partials)


def along_y(x, d):
    return lax.ppermute(x, "ctx", [(i, i - i % SIDE + (i + d) % SIDE) for i in range(SIDE * SIDE)])


def down_x(x, d):
    return lax.ppermute(x, "ctx", [(i, i - SIDE * d) for i in range(SIDE * d, SIDE * SIDE)])


def up_x(x, d):
    return lax.ppermute(x, "ctx", [(i, i + SIDE * d) for i in range(SIDE * SIDE - SIDE * d)])


def along_z(x, d):
    return lax.ppermute(x, "head", [(i, (i + 2 * d) % (2 * SIDE)) for i in range(2 * SIDE)])


def other_core(x):
    return lax.ppermute(x, "head", [(i, i ^ 1) for i in range(2 * SIDE)])


def body(queries, keys, values, house, rates, out_weight):
    rows = queries.shape[0]
    blocks = rows // C
    number = lax.axis_index("ctx")
    head = lax.axis_index("head")
    place = jnp.stack([number // SIDE, number % SIDE, head // 2, head % 2]).astype(jnp.int32)
    q, k, v, h = (x[:, 0, :] for x in (queries, keys, values, house))
    step, sent, passages, prefixes, applied, rights, finals, unit = transport(k, v, h, rates.reshape(blocks, C))
    steps = [step] + [along_y(step, d) for d in (1, 2, 3)]
    leaving, whole, suffixes, seens, starts = lead(place, q, prefixes, applied, unit, steps)
    first, third, second_link = down_x(leaving, 1), down_x(leaving, 3), down_x(whole, 2)
    before, after = along_y(sent, 1), along_y(sent, 3)
    moved, peak, total, summed, dealt = own(q, k, v, seens, starts, passages, rights, finals, out_weight)
    before, after, dealt = lax.optimization_barrier((before, after, dealt))
    columns = lax.all_to_all(dealt, "head", split_axis=0, concat_axis=0, tiled=True)
    shards = [sent, before, along_y(before[:rows], 1), along_y(after[rows:], 3), after]
    relayed, moved = lax.optimization_barrier((first, moved))
    second = down_x(relayed, 1)
    one, three = visitors(place, suffixes, shards, [(first, []), (third, [first, second_link])])
    second, one = lax.optimization_barrier((second, one))
    (two,) = visitors(place, suffixes, shards, [(second, [first])])
    returned = [up_x(one, 1), up_x(two, 2), up_x(three, 3)]
    own_row = row(place, moved, steps, shards)
    attended = merge(place, peak, total, summed, [own_row, *returned])
    half = rows // 2
    left_chip, right_chip = along_z(attended, 1), along_z(attended, 3)
    three_chips = jnp.stack([attended, left_chip, right_chip])
    upper, lower = along_z(left_chip[:half], 1), along_z(right_chip[half:], 3)

    def weights(core, offsets):
        return jnp.stack(
            [lax.dynamic_index_in_dim(columns, 2 * ((place[2] + d) % SIDE) + core, 0, False) for d in offsets]
        )

    def part(x, core, offsets):
        return jnp.einsum("srk,skn->rn", x, weights(core, offsets), preferred_element_type=F32)

    mine, theirs = place[3], 1 - place[3]
    projected = part(three_chips, mine, (0, SIDE - 1, 1))
    upper, lower, projected = lax.optimization_barrier((upper, lower, projected))
    across = jnp.concatenate([upper, lower], axis=0)
    projected = projected + part(other_core(three_chips), theirs, (0, SIDE - 1, 1))
    projected = projected + part(across[None], mine, (2,))
    projected = projected + part(other_core(across)[None], theirs, (2,))
    return (attended[:, None, :], projected.astype(BF16))


def solution(mesh):
    in_specs = (
        P("ctx", "head", None),
        P("ctx", "head", None),
        P("ctx", "head", None),
        P("ctx", "head", None),
        P("head", "ctx"),
        P("head", None),
    )
    out_specs = (P("ctx", "head", None), P("ctx", "head"))
    return jax.shard_map(body, mesh=mesh, in_specs=in_specs, out_specs=out_specs, check_vma=False)
```

```python
import jax
import jax.numpy as jnp
from jax import lax
from jax.experimental import pallas as pl
from jax.experimental.pallas import tpu as pltpu
from jax.sharding import PartitionSpec as P

C = 128
F32 = jnp.float32
BF16 = jnp.bfloat16
EPSILON = 1e-06
NEGATIVE = -1e30
LOG2E = 1.4426950408889634
VMEM_LIMIT = 56 * 1024 * 1024


def cost(microseconds):
    return pl.CostEstimate(flops=int(microseconds * 1.15e9), transcendentals=0, bytes_accessed=2**20)


def stacked(pair):
    return jnp.concatenate([pair, pair], axis=0)


def split(x):
    high = x.astype(BF16)
    return high, (x - high.astype(F32)).astype(BF16)


def left(x):
    return jnp.concatenate(split(x), axis=1)


def right_nn(x):
    pair = jnp.concatenate(split(x), axis=1)
    return jnp.concatenate([pair, pair], axis=0)


def right_nt(x):
    high, low = split(x)
    return jnp.concatenate(
        [jnp.concatenate([high, high], axis=1), jnp.concatenate([low, low], axis=1)], axis=0
    )


def halves(x):
    return x[:, : x.shape[1] // 2] + x[:, x.shape[1] // 2 :]


def nn(a, b):
    return halves(jnp.dot(a, b, preferred_element_type=F32))


def contract_last(a, b):
    return lax.dot_general(a, b, (((1,), (1,)), ((), ())), preferred_element_type=F32)


def nt(a, b):
    return halves(contract_last(a, b))


def unit_house(house):
    raw = house.astype(F32)
    return raw / jnp.sqrt(jnp.sum(raw * raw, axis=1, keepdims=True) + EPSILON)


def transport_kernel(keys, values, house, rates, step, sent, passages, prefixes, applied, rights, finals, unit):
    rows = keys.shape[0]
    sent[pl.ds(rows, rows), :] = values[...]
    blocks = rates.shape[0]
    row = lax.broadcasted_iota(jnp.int32, (C, C), 0)
    col = lax.broadcasted_iota(jnp.int32, (C, C), 1)
    eye = jnp.where(row == col, 1.0, 0.0).astype(F32)
    every = range(blocks)
    w = [unit_house(house[pl.ds(n * C, C), :]) for n in every]
    for n in every:
        unit[pl.ds(n * C, C), :] = w[n]
    wl = [left(x) for x in w]
    strict = []
    for n in every:
        gram = nt(wl[n], right_nt(w[n]))
        decay = jnp.transpose(jnp.broadcast_to(rates[n : n + 1, :], (C, C)))
        strict.append(jnp.where(row > col, gram, 0.0) * decay)
    x = [eye - jnp.where((row // 2) == (col // 2), strict[n], 0.0) for n in every]
    size = 2
    while size < C:
        band = ((row // (2 * size)) == (col // (2 * size))) & ((row // size) != (col // size))
        inner = [nn(left(jnp.where(band, strict[n], 0.0)), right_nn(x[n])) for n in every]
        x = [x[n] - nn(left(x[n]), right_nn(inner[n])) for n in every]
        size *= 2
    t = [x[n] * rates[n : n + 1, :] for n in every]
    final = []
    for n in every:
        k = keys[pl.ds(n * C, C), :]
        met = jnp.where(col > row, contract_last(jnp.concatenate([k, k], axis=1), wl[n]), 0.0)
        r = nt(left(met), right_nt(t[n]))
        rights[n] = r
        f = k.astype(F32) - nn(left(r), right_nn(w[n]))
        finals[pl.ds(n * C, C), :] = f
        final.append(f)
    passage = []
    for n in every:
        u = nn(left(t[n]), right_nn(w[n]))
        applied[n] = u
        passage.append(eye - nn(left(jnp.transpose(w[n])), right_nn(u)))
        passages[n] = passage[n]
    sent[pl.ds((blocks - 1) * C, C), :] = final[blocks - 1].astype(BF16)
    s = passage[blocks - 1]
    a = passage[0]
    prefixes[0] = left(eye)
    for n in range(blocks - 2, -1, -1):
        prefixes[blocks - 1 - n] = left(a)
        if n:
            a = nn(left(passage[blocks - 1 - n]), right_nn(a))
        sent[pl.ds(n * C, C), :] = nt(left(final[n]), right_nt(s)).astype(BF16)
        s = nn(left(s), right_nn(passage[n]))
    step[...] = left(s)


def transport(keys, values, house, rates):
    rows = keys.shape[0]
    blocks = rows // C
    square = jax.ShapeDtypeStruct((blocks, C, C), F32)
    flat = jax.ShapeDtypeStruct((rows, C), F32)
    return pl.pallas_call(
        transport_kernel,
        out_shape=(
            jax.ShapeDtypeStruct((C, 2 * C), BF16),
            jax.ShapeDtypeStruct((2 * rows, C), BF16),
            square,
            jax.ShapeDtypeStruct((blocks, C, 2 * C), BF16),
            square,
            square,
            flat,
            flat,
        ),
        cost_estimate=cost(8),
        compiler_params=pltpu.CompilerParams(vmem_limit_bytes=VMEM_LIMIT),
        name="transport",
    )(keys, values, house, rates)


SIDE = 4
COST_LEAD = 3
COST_OWN = 2
COST_VISIT = 3
COST_ROW = 6
COST_PAIR = 8


def lead_kernel(place, queries, prefixes, applied, unit, t0, t1, t2, t3, leaving, whole, suffixes, seens, starts, along, steps):
    blocks = applied.shape[0]
    rows = queries.shape[0]
    y = place[1]
    row = lax.broadcasted_iota(jnp.int32, (C, C), 0)
    col = lax.broadcasted_iota(jnp.int32, (C, C), 1)
    eye = jnp.where(row == col, 1.0, 0.0).astype(F32)
    along[...] = left(eye)
    for d, t in enumerate((t0, t1, t2, t3)):
        steps[lax.rem(y + (SIDE - d), SIDE)] = t[...]
        if d:

            @pl.when(y >= d)
            def _(t=t):
                along[...] = left(nn(along[...], stacked(t[...])))

    suffix = left(eye)
    for n in range(SIDE - 1, -1, -1):
        suffixes[lax.rem(y + (SIDE - n), SIDE)] = suffix
        suffix = left(nn(suffix, stacked(steps[n])))
    move = stacked(along[...])
    for n in range(blocks):
        here = pl.ds(n * C, C)
        q = queries[here, :].astype(F32) * (C**-0.5 * LOG2E)
        seen = left(jnp.where(row >= col, nt(left(q), right_nt(unit[here, :])), 0.0))
        start = left(q - nn(seen, right_nn(applied[n])))
        seens[here, :] = seen
        starts[here, :] = start
        out = left(nn(start, stacked(left(nn(prefixes[n], move)))))
        leaving[here, :] = out
    leaving[pl.ds(rows, C), :] = suffix
    whole[...] = suffix


def lead(place, queries, prefixes, applied, unit, steps):
    rows = queries.shape[0]
    pair = jax.ShapeDtypeStruct((rows, 2 * C), BF16)
    return pl.pallas_call(
        lead_kernel,
        out_shape=(
            jax.ShapeDtypeStruct((rows + C, 2 * C), BF16),
            jax.ShapeDtypeStruct((C, 2 * C), BF16),
            jax.ShapeDtypeStruct((SIDE, C, 2 * C), BF16),
            pair,
            pair,
        ),
        in_specs=[SCALARS] + [WHOLE] * (4 + SIDE),
        out_specs=(WHOLE,) * 5,
        scratch_shapes=[pltpu.VMEM((C, 2 * C), BF16), pltpu.VMEM((SIDE, C, 2 * C), BF16)],
        compiler_params=pltpu.CompilerParams(vmem_limit_bytes=VMEM_LIMIT),
        cost_estimate=cost(COST_LEAD),
        name="lead",
    )(place, queries, prefixes, applied, unit, *steps)


def own_kernel(
    queries, keys, values, seens, starts, passages, rights, finals, weight,
    moved, peak, total, summed, dealt, table, hand, sems
):
    blocks = passages.shape[0]
    pieces, _, width = dealt.shape
    taken = [
        pltpu.make_async_copy(weight.at[:, pl.ds(n * width, width)], hand.at[n], sems.at[0, n]) for n in range(pieces)
    ]
    given = [pltpu.make_async_copy(hand.at[n], dealt.at[n], sems.at[1, n]) for n in range(pieces)]
    for copy in taken:
        copy.start()
    row = lax.broadcasted_iota(jnp.int32, (C, C), 0)
    col = lax.broadcasted_iota(jnp.int32, (C, C), 1)
    for n in range(blocks):
        here = pl.ds(n * C, C)
        q = queries[here, :].astype(F32) * (C**-0.5 * LOG2E)
        k = keys[here, :]
        inside = contract_last(left(q), jnp.concatenate([k, k], axis=1)) - nt(seens[here, :], right_nt(rights[n]))
        table[here, here] = jnp.where(row >= col, inside, NEGATIVE)
        moved[here, :] = starts[here, :]
    for m in range(blocks - 2, -1, -1):
        here = pl.ds(m * C, C)
        after = pl.ds((m + 1) * C, (blocks - 1 - m) * C)
        block_rows = moved[after, :]
        table[after, here] = nt(block_rows, right_nt(finals[here, :]))
        moved[after, :] = left(nn(block_rows, right_nn(passages[m])))
    for n in range(pieces):
        taken[n].wait()
        given[n].start()
    for n in range(blocks):
        here = pl.ds(n * C, C)
        upto = pl.ds(0, (n + 1) * C)
        s = table[here, upto]
        m = jnp.max(s, axis=1, keepdims=True)
        p = jnp.exp2(s - m)
        peak[here, :] = jnp.broadcast_to(m, (C, C))
        total[here, :] = jnp.broadcast_to(jnp.sum(p, axis=1, keepdims=True), (C, C))
        summed[here, :] = jnp.dot(p.astype(BF16), values[upto, :], preferred_element_type=F32)
    for copy in given:
        copy.wait()


def own(queries, keys, values, seens, starts, passages, rights, finals, weight):
    rows = values.shape[0]
    pieces = 2 * SIDE
    dealt = (pieces, weight.shape[0], weight.shape[1] // pieces)
    flat = jax.ShapeDtypeStruct((rows, C), F32)
    return pl.pallas_call(
        own_kernel,
        out_shape=(
            jax.ShapeDtypeStruct((rows, 2 * C), BF16),
            flat,
            flat,
            flat,
            jax.ShapeDtypeStruct(dealt, weight.dtype),
        ),
        in_specs=[WHOLE] * 8 + [ANY],
        out_specs=(WHOLE,) * 4 + (ANY,),
        scratch_shapes=[
            pltpu.VMEM((rows, rows), F32),
            pltpu.VMEM(dealt, weight.dtype),
            pltpu.SemaphoreType.DMA((2, pieces)),
        ],
        compiler_params=pltpu.CompilerParams(vmem_limit_bytes=VMEM_LIMIT),
        cost_estimate=cost(COST_OWN),
        name="own",
    )(queries, keys, values, seens, starts, passages, rights, finals, weight)


ROWS = 512
LSE_ROWS = 32
ANY = pl.BlockSpec(memory_space=pl.ANY)
SCALARS = pl.BlockSpec(memory_space=pltpu.SMEM)
WHOLE = pl.BlockSpec(memory_space=pltpu.VMEM)


def meet(q, keys, values, state):
    rows = keys.shape[0]
    k = keys[...]
    v = values[...]
    s = contract_last(q, jnp.concatenate([k, k], axis=1))
    top = jnp.max(s, axis=1, keepdims=True)
    if state is None:
        new = jnp.broadcast_to(top, (q.shape[0], C))
    else:
        new = jnp.maximum(state[0], top)
    p = jnp.exp2(s - jnp.tile(new, (1, rows // C))).astype(BF16)
    pv = jnp.dot(p, jnp.concatenate([v, jnp.ones_like(v)], axis=1), preferred_element_type=F32)
    if state is None:
        return new, pv[:, C:], pv[:, :C]
    shrink = jnp.exp2(state[0] - new)
    return new, state[1] * shrink + pv[:, C:], state[2] * shrink + pv[:, :C]


def settle(out, mx, ls, acc):
    rows = mx.shape[0]
    row = lax.broadcasted_iota(jnp.int32, (C, C), 0)
    col = lax.broadcasted_iota(jnp.int32, (C, C), 1)
    out[pl.ds(0, rows), :] = (acc[...] / ls[...]).astype(BF16)
    lines = []
    for n in range(rows // C):
        here = pl.ds(n * C, C)
        lse = mx[here, :] + jnp.log2(ls[here, :])
        lines.append(jnp.sum(jnp.where(row == col, lse, 0.0), axis=0, keepdims=True))
    lse = jnp.concatenate(lines, axis=0)
    high = lse.astype(BF16).astype(F32)
    middle = (lse - high).astype(BF16).astype(F32)
    low = lse - high - middle
    out[pl.ds(rows, LSE_ROWS), :] = jnp.concatenate([high, middle, low, jnp.zeros_like(lse)], axis=0).astype(BF16)


def row_kernel(place, moved, t1, t2, s1, k2, v2, s3, out, mx, ls, acc, mv):
    y = place[1]
    rows = moved.shape[0]
    mv[...] = moved[...]
    parts = [(s.at[pl.ds(0, rows)], s.at[pl.ds(rows, rows)]) for s in (s1, s3)]
    parts.insert(1, (k2, v2))
    for d, (t, shard) in enumerate(zip((t1, t2, None), parts)):

        @pl.when(y > d)
        def _(d=d, t=t, shard=shard):
            for b in range(rows // ROWS):
                here = pl.ds(b * ROWS, ROWS)
                q = mv[here, :]
                state = (mx[here, :], ls[here, :], acc[here, :]) if d else None
                mx[here, :], ls[here, :], acc[here, :] = meet(q, *shard, state)
                if t is not None:
                    mv[here, :] = left(nn(q, stacked(t[...])))

    @pl.when(y > 0)
    def _():
        settle(out, mx, ls, acc)


def row(place, moved, steps, shards):
    rows = moved.shape[0]
    return pl.pallas_call(
        row_kernel,
        out_shape=jax.ShapeDtypeStruct((rows + LSE_ROWS, C), BF16),
        in_specs=[SCALARS] + [WHOLE] * 7,
        out_specs=WHOLE,
        scratch_shapes=[pltpu.VMEM((rows, C), F32)] * 3 + [pltpu.VMEM((rows, 2 * C), BF16)],
        compiler_params=pltpu.CompilerParams(vmem_limit_bytes=VMEM_LIMIT),
        cost_estimate=cost(COST_ROW),
        name="row",
    )(place, moved, steps[1], steps[2], *shards[1:])


def visit(out, query, moves, shards, mx, ls, acc):
    rows = mx.shape[0]
    for d in range(SIDE):
        for b in range(rows // ROWS):
            here = pl.ds(b * ROWS, ROWS)
            q = left(nn(query[here, :], stacked(moves[d])))
            state = None if d == 0 else (mx[here, :], ls[here, :], acc[here, :])
            mx[here, :], ls[here, :], acc[here, :] = meet(q, *shards[d], state)
    settle(out, mx, ls, acc)


def parted(s0, s1, k2, v2, s3):
    rows = k2.shape[0]
    return [(s0.at[pl.ds(0, rows)], s0.at[pl.ds(rows, rows)]), (s1.at[pl.ds(0, rows)], s1.at[pl.ds(rows, rows)])] + [
        (k2, v2),
        (s3.at[pl.ds(0, rows)], s3.at[pl.ds(rows, rows)]),
    ]


def pair_kernel(place, suffixes, s0, s1, k2, v2, s3, q1, q3, link1, link2, out1, out3, moves2, mx, ls, acc, moves3):
    shards = parted(s0, s1, k2, v2, s3)

    @pl.when(place[0] + 1 < SIDE)
    def _():
        one = link1[...]
        both = left(nn(link2[...], stacked(one)))
        for d in range(SIDE):
            move = stacked(suffixes[d])
            moves2[d] = left(nn(one, move))
            moves3[d] = left(nn(both, move))
        visit(out1, q1, suffixes, shards, mx, ls, acc)

    @pl.when(place[0] + 3 < SIDE)
    def _():
        visit(out3, q3, moves3, shards, mx, ls, acc)


def last_kernel(place, moves, s0, s1, k2, v2, s3, q2, out, mx, ls, acc):
    @pl.when(place[0] + 2 < SIDE)
    def _():
        visit(out, q2, moves, parted(s0, s1, k2, v2, s3), mx, ls, acc)


def visitors(place, suffixes, shards, queries, links):
    rows = queries[0].shape[0] - C
    back = jax.ShapeDtypeStruct((rows + LSE_ROWS, C), BF16)
    moves = (SIDE, C, 2 * C)
    specs = [pl.BlockSpec((rows, 2 * C), lambda i: (0, 0))] * len(queries)
    specs += [pl.BlockSpec((C, 2 * C), lambda i, n=link.shape[0] // C - 1: (n, 0)) for link in links]
    return pl.pallas_call(
        pair_kernel if links else last_kernel,
        out_shape=(back, back, jax.ShapeDtypeStruct(moves, BF16)) if links else back,
        grid=(1,),
        in_specs=[SCALARS] + [WHOLE] * (2 + SIDE) + specs,
        out_specs=(WHOLE,) * 3 if links else WHOLE,
        scratch_shapes=[pltpu.VMEM((rows, C), F32)] * 3 + ([pltpu.VMEM(moves, BF16)] if links else []),
        compiler_params=pltpu.CompilerParams(vmem_limit_bytes=VMEM_LIMIT),
        cost_estimate=cost(COST_PAIR if links else COST_VISIT),
        name="pair" if links else "last",
    )(place, suffixes, *shards, *queries, *links)


def merge_kernel(place, mx, ls, acc, own_row, r1, r2, r3, whole, *parts):
    rows = mx.shape[0]
    blocks = rows // C
    partials = ((own_row, place[1] > 0), (r1, place[0] > 0), (r2, place[0] > 1), (r3, place[0] > 2))
    lines = []
    for r, there in partials:
        tail = r[pl.ds(rows, LSE_ROWS), :].astype(F32)
        lse = tail[0:blocks] + tail[blocks : 2 * blocks] + tail[2 * blocks : 3 * blocks]
        lines.append(jnp.where(there, lse, NEGATIVE))
    for n in range(blocks):
        here = pl.ds(n * C, C)
        lse = [jnp.transpose(jnp.broadcast_to(line[n : n + 1, :], (C, C))) for line in lines]
        top = mx[here, :]
        for one in lse:
            top = jnp.maximum(top, one)
        share = jnp.exp2(mx[here, :] - top)
        total = ls[here, :] * share
        summed = acc[here, :] * share
        for one, (r, there) in zip(lse, partials):
            share = jnp.exp2(one - top)
            total += share
            summed += jnp.where(there, share * r[here, :].astype(F32), 0.0)
        done = (summed / total).astype(BF16)
        whole[here, :] = done
        each = blocks // len(parts)
        parts[n // each][pl.ds(n % each * C, C), :] = done


def merge(place, mx, ls, acc, partials):
    rows = mx.shape[0]
    return pl.pallas_call(
        merge_kernel,
        out_shape=(jax.ShapeDtypeStruct((rows, C), BF16),) + (jax.ShapeDtypeStruct((rows // 2, C), BF16),) * 2,
        in_specs=[SCALARS] + [WHOLE] * 7,
        out_specs=(WHOLE,) * 3,
        compiler_params=pltpu.CompilerParams(vmem_limit_bytes=VMEM_LIMIT),
        cost_estimate=cost(2),
        name="merge",
    )(place, mx, ls, acc, *partials)


def along_y(x, d):
    return lax.ppermute(x, "ctx", [(i, i - i % SIDE + (i + d) % SIDE) for i in range(SIDE * SIDE)])


def down_x(x, d):
    return lax.ppermute(x, "ctx", [(i, i - SIDE * d) for i in range(SIDE * d, SIDE * SIDE)])


def up_x(x, d):
    return lax.ppermute(x, "ctx", [(i, i + SIDE * d) for i in range(SIDE * SIDE - SIDE * d)])


def along_z(x, d):
    return lax.ppermute(x, "head", [(i, (i + 2 * d) % (2 * SIDE)) for i in range(2 * SIDE)])


def other_core(x):
    return lax.ppermute(x, "head", [(i, i ^ 1) for i in range(2 * SIDE)])


def body(queries, keys, values, house, rates, out_weight):
    rows = queries.shape[0]
    blocks = rows // C
    number = lax.axis_index("ctx")
    head = lax.axis_index("head")
    place = jnp.stack([number // SIDE, number % SIDE, head // 2, head % 2]).astype(jnp.int32)
    q, k, v, h = (x[:, 0, :] for x in (queries, keys, values, house))
    step, sent, passages, prefixes, applied, rights, finals, unit = transport(k, v, h, rates.reshape(blocks, C))
    steps = [step] + [along_y(step, d) for d in (1, 2, 3)]
    leaving, whole, suffixes, seens, starts = lead(place, q, prefixes, applied, unit, steps)
    first, third, second_link = down_x(leaving, 1), down_x(leaving, 3), down_x(whole, 2)
    before, after = along_y(sent, 1), along_y(sent, 3)
    moved, peak, total, summed, dealt = own(q, k, v, seens, starts, passages, rights, finals, out_weight)
    before, after, dealt = lax.optimization_barrier((before, after, dealt))
    columns = lax.all_to_all(dealt, "head", split_axis=0, concat_axis=0, tiled=True)
    shards = [sent, before, along_y(before[:rows], 1), along_y(after[rows:], 3), after]
    relayed, moved = lax.optimization_barrier((first, moved))
    second = down_x(relayed, 1)
    one, three, moves = visitors(place, suffixes, shards, [first, third], [first, second_link])
    two = visitors(place, moves, shards, [second], [])
    returned = [up_x(one, 1), up_x(two, 2), up_x(three, 3)]
    own_row = row(place, moved, steps, shards)
    attended, top, low = merge(place, peak, total, summed, [own_row, *returned])
    left_top, right_low = along_z(top, 1), along_z(low, 3)
    left_low, right_top = along_z(low, 1), along_z(top, 3)
    upper, lower = along_z(left_top, 1), along_z(right_low, 3)
    three_chips = jnp.concatenate([attended, left_top, left_low, right_top, right_low], axis=0).reshape(3, rows, C)

    def weights(core, offsets):
        return jnp.stack(
            [lax.dynamic_index_in_dim(columns, 2 * ((place[2] + d) % SIDE) + core, 0, False) for d in offsets]
        )

    def part(x, core, offsets):
        return jnp.einsum("srk,skn->rn", x, weights(core, offsets), preferred_element_type=F32)

    mine, theirs = place[3], 1 - place[3]
    three_across = other_core(three_chips)
    three_chips, upper, lower = lax.optimization_barrier((three_chips, upper, lower))
    across = jnp.concatenate([upper, lower], axis=0)
    projected = part(three_chips, mine, (0, SIDE - 1, 1)) + part(three_across, theirs, (0, SIDE - 1, 1))
    projected = projected + part(across[None], mine, (2,))
    projected = projected + part(other_core(across)[None], theirs, (2,))
    return (attended[:, None, :], projected.astype(BF16))


def solution(mesh):
    in_specs = (
        P("ctx", "head", None),
        P("ctx", "head", None),
        P("ctx", "head", None),
        P("ctx", "head", None),
        P("head", "ctx"),
        P("head", None),
    )
    out_specs = (P("ctx", "head", None), P("ctx", "head"))
    return jax.shard_map(body, mesh=mesh, in_specs=in_specs, out_specs=out_specs, check_vma=False)
```

```python
import jax
import jax.numpy as jnp
from jax import lax
from jax.experimental import pallas as pl
from jax.experimental.pallas import tpu as pltpu
from jax.sharding import PartitionSpec as P

C = 128
F32 = jnp.float32
BF16 = jnp.bfloat16
EPSILON = 1e-06
NEGATIVE = -1e30
LOG2E = 1.4426950408889634
VMEM_LIMIT = 56 * 1024 * 1024


def cost(microseconds):
    return pl.CostEstimate(flops=int(microseconds * 1.15e9), transcendentals=0, bytes_accessed=2**20)


def stacked(pair):
    return jnp.concatenate([pair, pair], axis=0)


def split(x):
    high = x.astype(BF16)
    return high, (x - high.astype(F32)).astype(BF16)


def left(x):
    return jnp.concatenate(split(x), axis=1)


def right_nn(x):
    pair = jnp.concatenate(split(x), axis=1)
    return jnp.concatenate([pair, pair], axis=0)


def right_nt(x):
    high, low = split(x)
    return jnp.concatenate(
        [jnp.concatenate([high, high], axis=1), jnp.concatenate([low, low], axis=1)], axis=0
    )


def halves(x):
    return x[:, : x.shape[1] // 2] + x[:, x.shape[1] // 2 :]


def nn(a, b):
    return halves(jnp.dot(a, b, preferred_element_type=F32))


def contract_last(a, b):
    return lax.dot_general(a, b, (((1,), (1,)), ((), ())), preferred_element_type=F32)


def nt(a, b):
    return halves(contract_last(a, b))


def unit_house(house):
    raw = house.astype(F32)
    return raw / jnp.sqrt(jnp.sum(raw * raw, axis=1, keepdims=True) + EPSILON)


def transport_kernel(keys, values, house, rates, step, sent, passages, prefixes, applied, rights, finals, unit):
    rows = keys.shape[0]
    sent[pl.ds(rows, rows), :] = values[...]
    blocks = rates.shape[0]
    row = lax.broadcasted_iota(jnp.int32, (C, C), 0)
    col = lax.broadcasted_iota(jnp.int32, (C, C), 1)
    eye = jnp.where(row == col, 1.0, 0.0).astype(F32)
    every = range(blocks)
    w = [unit_house(house[pl.ds(n * C, C), :]) for n in every]
    for n in every:
        unit[pl.ds(n * C, C), :] = w[n]
    wl = [left(x) for x in w]
    strict = []
    for n in every:
        gram = nt(wl[n], right_nt(w[n]))
        decay = jnp.transpose(jnp.broadcast_to(rates[n : n + 1, :], (C, C)))
        strict.append(jnp.where(row > col, gram, 0.0) * decay)
    x = [eye - jnp.where((row // 2) == (col // 2), strict[n], 0.0) for n in every]
    size = 2
    while size < C:
        band = ((row // (2 * size)) == (col // (2 * size))) & ((row // size) != (col // size))
        inner = [nn(left(jnp.where(band, strict[n], 0.0)), right_nn(x[n])) for n in every]
        x = [x[n] - nn(left(x[n]), right_nn(inner[n])) for n in every]
        size *= 2
    t = [x[n] * rates[n : n + 1, :] for n in every]
    final = []
    for n in every:
        k = keys[pl.ds(n * C, C), :]
        met = jnp.where(col > row, contract_last(jnp.concatenate([k, k], axis=1), wl[n]), 0.0)
        r = nt(left(met), right_nt(t[n]))
        rights[n] = r
        f = k.astype(F32) - nn(left(r), right_nn(w[n]))
        finals[pl.ds(n * C, C), :] = f
        final.append(f)
    passage = []
    for n in every:
        u = nn(left(t[n]), right_nn(w[n]))
        applied[n] = u
        passage.append(eye - nn(left(jnp.transpose(w[n])), right_nn(u)))
        passages[n] = passage[n]
    sent[pl.ds((blocks - 1) * C, C), :] = final[blocks - 1].astype(BF16)
    s = passage[blocks - 1]
    a = passage[0]
    prefixes[0] = left(eye)
    for n in range(blocks - 2, -1, -1):
        prefixes[blocks - 1 - n] = left(a)
        if n:
            a = nn(left(passage[blocks - 1 - n]), right_nn(a))
        sent[pl.ds(n * C, C), :] = nt(left(final[n]), right_nt(s)).astype(BF16)
        s = nn(left(s), right_nn(passage[n]))
    step[...] = left(s)


def transport(keys, values, house, rates):
    rows = keys.shape[0]
    blocks = rows // C
    square = jax.ShapeDtypeStruct((blocks, C, C), F32)
    flat = jax.ShapeDtypeStruct((rows, C), F32)
    return pl.pallas_call(
        transport_kernel,
        out_shape=(
            jax.ShapeDtypeStruct((C, 2 * C), BF16),
            jax.ShapeDtypeStruct((2 * rows, C), BF16),
            square,
            jax.ShapeDtypeStruct((blocks, C, 2 * C), BF16),
            square,
            square,
            flat,
            flat,
        ),
        cost_estimate=cost(8),
        compiler_params=pltpu.CompilerParams(vmem_limit_bytes=VMEM_LIMIT),
        name="transport",
    )(keys, values, house, rates)


SIDE = 4
COST_LEAD = 3
COST_OWN = 2
COST_VISIT = 3
COST_ROW = 6
COST_PAIR = 8


def lead_kernel(place, queries, prefixes, applied, unit, t0, t1, t2, t3, leaving, whole, suffixes, seens, starts, along, steps):
    blocks = applied.shape[0]
    rows = queries.shape[0]
    y = place[1]
    row = lax.broadcasted_iota(jnp.int32, (C, C), 0)
    col = lax.broadcasted_iota(jnp.int32, (C, C), 1)
    eye = jnp.where(row == col, 1.0, 0.0).astype(F32)
    along[...] = left(eye)
    for d, t in enumerate((t0, t1, t2, t3)):
        steps[lax.rem(y + (SIDE - d), SIDE)] = t[...]
        if d:

            @pl.when(y >= d)
            def _(t=t):
                along[...] = left(nn(along[...], stacked(t[...])))

    suffix = left(eye)
    for n in range(SIDE - 1, -1, -1):
        suffixes[lax.rem(y + (SIDE - n), SIDE)] = suffix
        suffix = left(nn(suffix, stacked(steps[n])))
    move = stacked(along[...])
    for n in range(blocks):
        here = pl.ds(n * C, C)
        q = queries[here, :].astype(F32) * (C**-0.5 * LOG2E)
        seen = left(jnp.where(row >= col, nt(left(q), right_nt(unit[here, :])), 0.0))
        start = left(q - nn(seen, right_nn(applied[n])))
        seens[here, :] = seen
        starts[here, :] = start
        out = left(nn(start, stacked(left(nn(prefixes[n], move)))))
        leaving[here, :] = out
    leaving[pl.ds(rows, C), :] = suffix
    whole[...] = suffix


def lead(place, queries, prefixes, applied, unit, steps):
    rows = queries.shape[0]
    pair = jax.ShapeDtypeStruct((rows, 2 * C), BF16)
    return pl.pallas_call(
        lead_kernel,
        out_shape=(
            jax.ShapeDtypeStruct((rows + C, 2 * C), BF16),
            jax.ShapeDtypeStruct((C, 2 * C), BF16),
            jax.ShapeDtypeStruct((SIDE, C, 2 * C), BF16),
            pair,
            pair,
        ),
        in_specs=[SCALARS] + [WHOLE] * (4 + SIDE),
        out_specs=(WHOLE,) * 5,
        scratch_shapes=[pltpu.VMEM((C, 2 * C), BF16), pltpu.VMEM((SIDE, C, 2 * C), BF16)],
        compiler_params=pltpu.CompilerParams(vmem_limit_bytes=VMEM_LIMIT),
        cost_estimate=cost(COST_LEAD),
        name="lead",
    )(place, queries, prefixes, applied, unit, *steps)


def own_kernel(
    queries, keys, values, seens, starts, passages, rights, finals, weight,
    moved, out, dealt, table, peak, total, summed, hand, sems
):
    blocks = passages.shape[0]
    pieces, _, width = dealt.shape
    taken = [
        pltpu.make_async_copy(weight.at[:, pl.ds(n * width, width)], hand.at[n], sems.at[0, n]) for n in range(pieces)
    ]
    given = [pltpu.make_async_copy(hand.at[n], dealt.at[n], sems.at[1, n]) for n in range(pieces)]
    for copy in taken:
        copy.start()
    row = lax.broadcasted_iota(jnp.int32, (C, C), 0)
    col = lax.broadcasted_iota(jnp.int32, (C, C), 1)
    for n in range(blocks):
        here = pl.ds(n * C, C)
        q = queries[here, :].astype(F32) * (C**-0.5 * LOG2E)
        k = keys[here, :]
        inside = contract_last(left(q), jnp.concatenate([k, k], axis=1)) - nt(seens[here, :], right_nt(rights[n]))
        table[here, here] = jnp.where(row >= col, inside, NEGATIVE)
        moved[here, :] = starts[here, :]
    for m in range(blocks - 2, -1, -1):
        here = pl.ds(m * C, C)
        after = pl.ds((m + 1) * C, (blocks - 1 - m) * C)
        block_rows = moved[after, :]
        table[after, here] = nt(block_rows, right_nt(finals[here, :]))
        moved[after, :] = left(nn(block_rows, right_nn(passages[m])))
    for n in range(pieces):
        taken[n].wait()
        given[n].start()
    for n in range(blocks):
        here = pl.ds(n * C, C)
        upto = pl.ds(0, (n + 1) * C)
        s = table[here, upto]
        m = jnp.max(s, axis=1, keepdims=True)
        p = jnp.exp2(s - m)
        peak[here, :] = jnp.broadcast_to(m, (C, C))
        total[here, :] = jnp.broadcast_to(jnp.sum(p, axis=1, keepdims=True), (C, C))
        summed[here, :] = jnp.dot(p.astype(BF16), values[upto, :], preferred_element_type=F32)
    settle(out, peak, total, summed)
    for copy in given:
        copy.wait()


def own(queries, keys, values, seens, starts, passages, rights, finals, weight):
    rows = values.shape[0]
    pieces = 2 * SIDE
    dealt = (pieces, weight.shape[0], weight.shape[1] // pieces)
    return pl.pallas_call(
        own_kernel,
        out_shape=(
            jax.ShapeDtypeStruct((rows, 2 * C), BF16),
            jax.ShapeDtypeStruct((rows + LSE_ROWS, C), BF16),
            jax.ShapeDtypeStruct(dealt, weight.dtype),
        ),
        in_specs=[WHOLE] * 8 + [ANY],
        out_specs=(WHOLE, WHOLE, ANY),
        scratch_shapes=[
            pltpu.VMEM((rows, rows), F32),
            pltpu.VMEM((rows, C), F32),
            pltpu.VMEM((rows, C), F32),
            pltpu.VMEM((rows, C), F32),
            pltpu.VMEM(dealt, weight.dtype),
            pltpu.SemaphoreType.DMA((2, pieces)),
        ],
        compiler_params=pltpu.CompilerParams(vmem_limit_bytes=VMEM_LIMIT),
        cost_estimate=cost(COST_OWN),
        name="own",
    )(queries, keys, values, seens, starts, passages, rights, finals, weight)


ROWS = 512
LSE_ROWS = 32
ANY = pl.BlockSpec(memory_space=pl.ANY)
SCALARS = pl.BlockSpec(memory_space=pltpu.SMEM)
WHOLE = pl.BlockSpec(memory_space=pltpu.VMEM)


def meet(q, keys, values, state):
    rows = keys.shape[0]
    k = keys[...]
    v = values[...]
    s = contract_last(q, jnp.concatenate([k, k], axis=1))
    top = jnp.max(s, axis=1, keepdims=True)
    if state is None:
        new = jnp.broadcast_to(top, (q.shape[0], C))
    else:
        new = jnp.maximum(state[0], top)
    p = jnp.exp2(s - jnp.tile(new, (1, rows // C))).astype(BF16)
    pv = jnp.dot(p, jnp.concatenate([v, jnp.ones_like(v)], axis=1), preferred_element_type=F32)
    if state is None:
        return new, pv[:, C:], pv[:, :C]
    shrink = jnp.exp2(state[0] - new)
    return new, state[1] * shrink + pv[:, C:], state[2] * shrink + pv[:, :C]


def settle(out, mx, ls, acc):
    rows = mx.shape[0]
    row = lax.broadcasted_iota(jnp.int32, (C, C), 0)
    col = lax.broadcasted_iota(jnp.int32, (C, C), 1)
    out[pl.ds(0, rows), :] = (acc[...] / ls[...]).astype(BF16)
    lines = []
    for n in range(rows // C):
        here = pl.ds(n * C, C)
        lse = mx[here, :] + jnp.log2(ls[here, :])
        lines.append(jnp.sum(jnp.where(row == col, lse, 0.0), axis=0, keepdims=True))
    lse = jnp.concatenate(lines, axis=0)
    high = lse.astype(BF16).astype(F32)
    middle = (lse - high).astype(BF16).astype(F32)
    low = lse - high - middle
    out[pl.ds(rows, LSE_ROWS), :] = jnp.concatenate([high, middle, low, jnp.zeros_like(lse)], axis=0).astype(BF16)


def row_kernel(place, moved, t1, t2, s1, k2, v2, s3, out, mx, ls, acc, mv):
    y = place[1]
    rows = moved.shape[0]
    parts = [(s.at[pl.ds(0, rows)], s.at[pl.ds(rows, rows)]) for s in (s1, s3)]
    parts.insert(1, (k2, v2))
    for count in range(1, SIDE):

        @pl.when(y == count)
        def _(count=count):
            for d, (t, shard) in enumerate(zip((t1, t2, None)[:count], parts)):
                for b in range(rows // ROWS):
                    here = pl.ds(b * ROWS, ROWS)
                    q = mv[here, :] if d else moved[here, :]
                    state = (mx[here, :], ls[here, :], acc[here, :]) if d else None
                    mx[here, :], ls[here, :], acc[here, :] = meet(q, *shard, state)
                    if d + 1 < count:
                        mv[here, :] = left(nn(q, stacked(t[...])))
            settle(out, mx, ls, acc)


def row(place, moved, steps, shards):
    rows = moved.shape[0]
    return pl.pallas_call(
        row_kernel,
        out_shape=jax.ShapeDtypeStruct((rows + LSE_ROWS, C), BF16),
        in_specs=[SCALARS] + [WHOLE] * 7,
        out_specs=WHOLE,
        scratch_shapes=[pltpu.VMEM((rows, C), F32)] * 3 + [pltpu.VMEM((rows, 2 * C), BF16)],
        compiler_params=pltpu.CompilerParams(vmem_limit_bytes=VMEM_LIMIT),
        cost_estimate=cost(COST_ROW),
        name="row",
    )(place, moved, steps[1], steps[2], *shards[1:])


def visit(out, query, moves, shards, mx, ls, acc):
    rows = mx.shape[0]
    for d in range(SIDE):
        for b in range(rows // ROWS):
            here = pl.ds(b * ROWS, ROWS)
            q = left(nn(query[here, :], stacked(moves[d])))
            state = None if d == 0 else (mx[here, :], ls[here, :], acc[here, :])
            mx[here, :], ls[here, :], acc[here, :] = meet(q, *shards[d], state)
    settle(out, mx, ls, acc)


def parted(s0, s1, k2, v2, s3):
    rows = k2.shape[0]
    return [(s0.at[pl.ds(0, rows)], s0.at[pl.ds(rows, rows)]), (s1.at[pl.ds(0, rows)], s1.at[pl.ds(rows, rows)])] + [
        (k2, v2),
        (s3.at[pl.ds(0, rows)], s3.at[pl.ds(rows, rows)]),
    ]


def pair_kernel(place, suffixes, s0, s1, k2, v2, s3, q1, q3, link1, link2, out1, out3, moves2, mx, ls, acc, moves3):
    shards = parted(s0, s1, k2, v2, s3)

    @pl.when(place[0] + 1 < SIDE)
    def _():
        one = link1[...]
        both = left(nn(link2[...], stacked(one)))
        for d in range(SIDE):
            move = stacked(suffixes[d])
            moves2[d] = left(nn(one, move))
            moves3[d] = left(nn(both, move))
        visit(out1, q1, suffixes, shards, mx, ls, acc)

    @pl.when(place[0] + 3 < SIDE)
    def _():
        visit(out3, q3, moves3, shards, mx, ls, acc)


def last_kernel(place, moves, s0, s1, k2, v2, s3, q2, out, mx, ls, acc):
    @pl.when(place[0] + 2 < SIDE)
    def _():
        visit(out, q2, moves, parted(s0, s1, k2, v2, s3), mx, ls, acc)


def visitors(place, suffixes, shards, queries, links):
    rows = queries[0].shape[0] - C
    back = jax.ShapeDtypeStruct((rows + LSE_ROWS, C), BF16)
    moves = (SIDE, C, 2 * C)
    specs = [pl.BlockSpec((rows, 2 * C), lambda i: (0, 0))] * len(queries)
    specs += [pl.BlockSpec((C, 2 * C), lambda i, n=link.shape[0] // C - 1: (n, 0)) for link in links]
    return pl.pallas_call(
        pair_kernel if links else last_kernel,
        out_shape=(back, back, jax.ShapeDtypeStruct(moves, BF16)) if links else back,
        grid=(1,),
        in_specs=[SCALARS] + [WHOLE] * (2 + SIDE) + specs,
        out_specs=(WHOLE,) * 3 if links else WHOLE,
        scratch_shapes=[pltpu.VMEM((rows, C), F32)] * 3 + ([pltpu.VMEM(moves, BF16)] if links else []),
        compiler_params=pltpu.CompilerParams(vmem_limit_bytes=VMEM_LIMIT),
        cost_estimate=cost(COST_PAIR if links else COST_VISIT),
        name="pair" if links else "last",
    )(place, suffixes, *shards, *queries, *links)


def merge_kernel(place, inside, own_row, r1, r2, r3, whole, *parts):
    rows = whole.shape[0]
    blocks = rows // C
    partials = ((inside, None), (own_row, place[1] > 0), (r1, place[0] > 0), (r2, place[0] > 1), (r3, place[0] > 2))
    lines = []
    for r, there in partials:
        tail = r[pl.ds(rows, LSE_ROWS), :].astype(F32)
        lse = tail[0:blocks] + tail[blocks : 2 * blocks] + tail[2 * blocks : 3 * blocks]
        lines.append(lse if there is None else jnp.where(there, lse, NEGATIVE))
    top = lines[0]
    for line in lines[1:]:
        top = jnp.maximum(top, line)
    shares = [jnp.exp2(line - top) for line in lines]
    total = shares[0] + shares[1] + shares[2] + shares[3] + shares[4]
    shares = [share / total for share in shares]
    for n in range(blocks):
        here = pl.ds(n * C, C)
        summed = None
        for share, (r, there) in zip(shares, partials):
            one = jnp.transpose(jnp.broadcast_to(share[n : n + 1, :], (C, C))) * r[here, :].astype(F32)
            summed = one if there is None else summed + jnp.where(there, one, 0.0)
        done = summed.astype(BF16)
        whole[here, :] = done
        each = blocks // len(parts)
        parts[n // each][pl.ds(n % each * C, C), :] = done


def merge(place, partials):
    rows = partials[0].shape[0] - LSE_ROWS
    return pl.pallas_call(
        merge_kernel,
        out_shape=(jax.ShapeDtypeStruct((rows, C), BF16),) + (jax.ShapeDtypeStruct((rows // 2, C), BF16),) * 2,
        in_specs=[SCALARS] + [WHOLE] * 5,
        out_specs=(WHOLE,) * 3,
        compiler_params=pltpu.CompilerParams(vmem_limit_bytes=VMEM_LIMIT),
        cost_estimate=cost(2),
        name="merge",
    )(place, *partials)


def along_y(x, d):
    return lax.ppermute(x, "ctx", [(i, i - i % SIDE + (i + d) % SIDE) for i in range(SIDE * SIDE)])


def down_x(x, d):
    return lax.ppermute(x, "ctx", [(i, i - SIDE * d) for i in range(SIDE * d, SIDE * SIDE)])


def up_x(x, d):
    return lax.ppermute(x, "ctx", [(i, i + SIDE * d) for i in range(SIDE * SIDE - SIDE * d)])


def along_z(x, d):
    return lax.ppermute(x, "head", [(i, (i + 2 * d) % (2 * SIDE)) for i in range(2 * SIDE)])


def other_core(x):
    return lax.ppermute(x, "head", [(i, i ^ 1) for i in range(2 * SIDE)])


def body(queries, keys, values, house, rates, out_weight):
    rows = queries.shape[0]
    blocks = rows // C
    number = lax.axis_index("ctx")
    head = lax.axis_index("head")
    place = jnp.stack([number // SIDE, number % SIDE, head // 2, head % 2]).astype(jnp.int32)
    q, k, v, h = (x[:, 0, :] for x in (queries, keys, values, house))
    step, sent, passages, prefixes, applied, rights, finals, unit = transport(k, v, h, rates.reshape(blocks, C))
    steps = [step] + [along_y(step, d) for d in (1, 2, 3)]
    leaving, whole, suffixes, seens, starts = lead(place, q, prefixes, applied, unit, steps)
    first, third, second_link = down_x(leaving, 1), down_x(leaving, 3), down_x(whole, 2)
    before, after = along_y(sent, 1), along_y(sent, 3)
    moved, inside, dealt = own(q, k, v, seens, starts, passages, rights, finals, out_weight)
    before, after, dealt = lax.optimization_barrier((before, after, dealt))
    columns = lax.all_to_all(dealt, "head", split_axis=0, concat_axis=0, tiled=True)
    shards = [sent, before, along_y(before[:rows], 1), along_y(after[rows:], 3), after]
    relayed, moved = lax.optimization_barrier((first, moved))
    second = down_x(relayed, 1)
    one, three, moves = visitors(place, suffixes, shards, [first, third], [first, second_link])
    two = visitors(place, moves, shards, [second], [])
    returned = [up_x(one, 1), up_x(two, 2), up_x(three, 3)]
    own_row = row(place, moved, steps, shards)
    attended, top, low = merge(place, [inside, own_row, *returned])
    left_top, right_low = along_z(top, 1), along_z(low, 3)
    left_low, right_top = along_z(low, 1), along_z(top, 3)
    upper, lower = along_z(left_top, 1), along_z(right_low, 3)
    three_chips = jnp.concatenate([attended, left_top, left_low, right_top, right_low], axis=0).reshape(3, rows, C)

    def weights(core, offsets):
        return jnp.stack(
            [lax.dynamic_index_in_dim(columns, 2 * ((place[2] + d) % SIDE) + core, 0, False) for d in offsets]
        )

    def part(x, core, offsets):
        return jnp.einsum("srk,skn->rn", x, weights(core, offsets), preferred_element_type=F32)

    mine, theirs = place[3], 1 - place[3]
    three_across = other_core(three_chips)
    three_chips, upper, lower = lax.optimization_barrier((three_chips, upper, lower))
    across = jnp.concatenate([upper, lower], axis=0)
    projected = part(three_chips, mine, (0, SIDE - 1, 1)) + part(three_across, theirs, (0, SIDE - 1, 1))
    projected = projected + part(across[None], mine, (2,))
    projected = projected + part(other_core(across)[None], theirs, (2,))
    return (attended[:, None, :], projected.astype(BF16))


def solution(mesh):
    in_specs = (
        P("ctx", "head", None),
        P("ctx", "head", None),
        P("ctx", "head", None),
        P("ctx", "head", None),
        P("head", "ctx"),
        P("head", None),
    )
    out_specs = (P("ctx", "head", None), P("ctx", "head"))
    return jax.shard_map(body, mesh=mesh, in_specs=in_specs, out_specs=out_specs, check_vma=False)
```

```python
import jax
import jax.numpy as jnp
from jax import lax
from jax.experimental import pallas as pl
from jax.experimental.pallas import tpu as pltpu
from jax.sharding import PartitionSpec as P

C = 128
F32 = jnp.float32
BF16 = jnp.bfloat16
EPSILON = 1e-06
NEGATIVE = -1e30
LOG2E = 1.4426950408889634
VMEM_LIMIT = 56 * 1024 * 1024


def cost(microseconds):
    return pl.CostEstimate(flops=int(microseconds * 1.15e9), transcendentals=0, bytes_accessed=2**20)


def stacked(pair):
    return jnp.concatenate([pair, pair], axis=0)


def split(x):
    high = x.astype(BF16)
    return high, (x - high.astype(F32)).astype(BF16)


def left(x):
    return jnp.concatenate(split(x), axis=1)


def right_nn(x):
    pair = jnp.concatenate(split(x), axis=1)
    return jnp.concatenate([pair, pair], axis=0)


def right_nt(x):
    high, low = split(x)
    return jnp.concatenate(
        [jnp.concatenate([high, high], axis=1), jnp.concatenate([low, low], axis=1)], axis=0
    )


def halves(x):
    return x[:, : x.shape[1] // 2] + x[:, x.shape[1] // 2 :]


def nn(a, b):
    return halves(jnp.dot(a, b, preferred_element_type=F32))


def contract_last(a, b):
    return lax.dot_general(a, b, (((1,), (1,)), ((), ())), preferred_element_type=F32)


def nt(a, b):
    return halves(contract_last(a, b))


def unit_house(house):
    raw = house.astype(F32)
    return raw / jnp.sqrt(jnp.sum(raw * raw, axis=1, keepdims=True) + EPSILON)


def transport_kernel(keys, values, house, rates, step, sent, passages, prefixes, applied, rights, finals, unit):
    rows = keys.shape[0]
    sent[pl.ds(rows, rows), :] = values[...]
    blocks = rates.shape[0]
    row = lax.broadcasted_iota(jnp.int32, (C, C), 0)
    col = lax.broadcasted_iota(jnp.int32, (C, C), 1)
    eye = jnp.where(row == col, 1.0, 0.0).astype(F32)
    every = range(blocks)
    w = [unit_house(house[pl.ds(n * C, C), :]) for n in every]
    for n in every:
        unit[pl.ds(n * C, C), :] = w[n]
    wl = [left(x) for x in w]
    strict = []
    for n in every:
        gram = nt(wl[n], right_nt(w[n]))
        decay = jnp.transpose(jnp.broadcast_to(rates[n : n + 1, :], (C, C)))
        strict.append(jnp.where(row > col, gram, 0.0) * decay)
    x = [eye - jnp.where((row // 2) == (col // 2), strict[n], 0.0) for n in every]
    size = 2
    while size < C:
        band = ((row // (2 * size)) == (col // (2 * size))) & ((row // size) != (col // size))
        inner = [nn(left(jnp.where(band, strict[n], 0.0)), right_nn(x[n])) for n in every]
        x = [x[n] - nn(left(x[n]), right_nn(inner[n])) for n in every]
        size *= 2
    t = [x[n] * rates[n : n + 1, :] for n in every]
    final = []
    for n in every:
        k = keys[pl.ds(n * C, C), :]
        met = jnp.where(col > row, contract_last(jnp.concatenate([k, k], axis=1), wl[n]), 0.0)
        r = nt(left(met), right_nt(t[n]))
        rights[n] = r
        f = k.astype(F32) - nn(left(r), right_nn(w[n]))
        finals[pl.ds(n * C, C), :] = f
        final.append(f)
    passage = []
    for n in every:
        u = nn(left(t[n]), right_nn(w[n]))
        applied[n] = u
        passage.append(eye - nn(left(jnp.transpose(w[n])), right_nn(u)))
        passages[n] = passage[n]
    sent[pl.ds((blocks - 1) * C, C), :] = final[blocks - 1].astype(BF16)
    s = passage[blocks - 1]
    a = passage[0]
    prefixes[0] = left(eye)
    for n in range(blocks - 2, -1, -1):
        prefixes[blocks - 1 - n] = left(a)
        if n:
            a = nn(left(passage[blocks - 1 - n]), right_nn(a))
        sent[pl.ds(n * C, C), :] = nt(left(final[n]), right_nt(s)).astype(BF16)
        s = nn(left(s), right_nn(passage[n]))
    step[...] = left(s)


def transport(keys, values, house, rates):
    rows = keys.shape[0]
    blocks = rows // C
    square = jax.ShapeDtypeStruct((blocks, C, C), F32)
    flat = jax.ShapeDtypeStruct((rows, C), F32)
    return pl.pallas_call(
        transport_kernel,
        out_shape=(
            jax.ShapeDtypeStruct((C, 2 * C), BF16),
            jax.ShapeDtypeStruct((2 * rows, C), BF16),
            square,
            jax.ShapeDtypeStruct((blocks, C, 2 * C), BF16),
            square,
            square,
            flat,
            flat,
        ),
        cost_estimate=cost(8),
        compiler_params=pltpu.CompilerParams(vmem_limit_bytes=VMEM_LIMIT),
        name="transport",
    )(keys, values, house, rates)


SIDE = 4
COST_LEAD = 3
COST_OWN = 2
COST_VISIT = 3
COST_ROW = 6
COST_PAIR = 8


def lead_kernel(place, queries, prefixes, applied, unit, t0, t1, t2, t3, leaving, whole, suffixes, seens, starts, along, steps):
    blocks = applied.shape[0]
    rows = queries.shape[0]
    y = place[1]
    row = lax.broadcasted_iota(jnp.int32, (C, C), 0)
    col = lax.broadcasted_iota(jnp.int32, (C, C), 1)
    eye = jnp.where(row == col, 1.0, 0.0).astype(F32)
    along[...] = left(eye)
    for d, t in enumerate((t0, t1, t2, t3)):
        steps[lax.rem(y + (SIDE - d), SIDE)] = t[...]
        if d:

            @pl.when(y >= d)
            def _(t=t):
                along[...] = left(nn(along[...], stacked(t[...])))

    suffix = left(eye)
    for n in range(SIDE - 1, -1, -1):
        suffixes[lax.rem(y + (SIDE - n), SIDE)] = suffix
        suffix = left(nn(suffix, stacked(steps[n])))
    move = stacked(along[...])
    for n in range(blocks):
        here = pl.ds(n * C, C)
        q = queries[here, :].astype(F32) * (C**-0.5 * LOG2E)
        seen = left(jnp.where(row >= col, nt(left(q), right_nt(unit[here, :])), 0.0))
        start = left(q - nn(seen, right_nn(applied[n])))
        seens[here, :] = seen
        starts[here, :] = start
        out = left(nn(start, stacked(left(nn(prefixes[n], move)))))
        leaving[here, :] = out
    leaving[pl.ds(rows, C), :] = suffix
    whole[...] = suffix


def lead(place, queries, prefixes, applied, unit, steps):
    rows = queries.shape[0]
    pair = jax.ShapeDtypeStruct((rows, 2 * C), BF16)
    return pl.pallas_call(
        lead_kernel,
        out_shape=(
            jax.ShapeDtypeStruct((rows + C, 2 * C), BF16),
            jax.ShapeDtypeStruct((C, 2 * C), BF16),
            jax.ShapeDtypeStruct((SIDE, C, 2 * C), BF16),
            pair,
            pair,
        ),
        in_specs=[SCALARS] + [WHOLE] * (4 + SIDE),
        out_specs=(WHOLE,) * 5,
        scratch_shapes=[pltpu.VMEM((C, 2 * C), BF16), pltpu.VMEM((SIDE, C, 2 * C), BF16)],
        compiler_params=pltpu.CompilerParams(vmem_limit_bytes=VMEM_LIMIT),
        cost_estimate=cost(COST_LEAD),
        name="lead",
    )(place, queries, prefixes, applied, unit, *steps)


def own_kernel(
    queries, keys, values, seens, starts, passages, rights, finals, weight,
    moved, out, dealt, table, peak, total, summed, hand, sems
):
    blocks = passages.shape[0]
    pieces, _, width = dealt.shape
    taken = [
        pltpu.make_async_copy(weight.at[:, pl.ds(n * width, width)], hand.at[n], sems.at[0, n]) for n in range(pieces)
    ]
    given = [pltpu.make_async_copy(hand.at[n], dealt.at[n], sems.at[1, n]) for n in range(pieces)]
    for copy in taken:
        copy.start()
    row = lax.broadcasted_iota(jnp.int32, (C, C), 0)
    col = lax.broadcasted_iota(jnp.int32, (C, C), 1)
    for n in range(blocks):
        here = pl.ds(n * C, C)
        q = queries[here, :].astype(F32) * (C**-0.5 * LOG2E)
        k = keys[here, :]
        inside = contract_last(left(q), jnp.concatenate([k, k], axis=1)) - nt(seens[here, :], right_nt(rights[n]))
        table[here, here] = jnp.where(row >= col, inside, NEGATIVE)
        moved[here, :] = starts[here, :]
    for m in range(blocks - 2, -1, -1):
        here = pl.ds(m * C, C)
        after = pl.ds((m + 1) * C, (blocks - 1 - m) * C)
        block_rows = moved[after, :]
        table[after, here] = nt(block_rows, right_nt(finals[here, :]))
        moved[after, :] = left(nn(block_rows, right_nn(passages[m])))
    for n in range(pieces):
        taken[n].wait()
        given[n].start()
    for n in range(blocks):
        here = pl.ds(n * C, C)
        upto = pl.ds(0, (n + 1) * C)
        s = table[here, upto]
        m = jnp.max(s, axis=1, keepdims=True)
        p = jnp.exp2(s - m)
        peak[here, :] = jnp.broadcast_to(m, (C, C))
        total[here, :] = jnp.broadcast_to(jnp.sum(p, axis=1, keepdims=True), (C, C))
        summed[here, :] = jnp.dot(p.astype(BF16), values[upto, :], preferred_element_type=F32)
    settle(out, peak, total, summed)
    for copy in given:
        copy.wait()


def own(queries, keys, values, seens, starts, passages, rights, finals, weight):
    rows = values.shape[0]
    pieces = 2 * SIDE
    dealt = (pieces, weight.shape[0], weight.shape[1] // pieces)
    return pl.pallas_call(
        own_kernel,
        out_shape=(
            jax.ShapeDtypeStruct((rows, 2 * C), BF16),
            jax.ShapeDtypeStruct((rows + LSE_ROWS, C), BF16),
            jax.ShapeDtypeStruct(dealt, weight.dtype),
        ),
        in_specs=[WHOLE] * 8 + [ANY],
        out_specs=(WHOLE, WHOLE, ANY),
        scratch_shapes=[
            pltpu.VMEM((rows, rows), F32),
            pltpu.VMEM((rows, C), F32),
            pltpu.VMEM((rows, C), F32),
            pltpu.VMEM((rows, C), F32),
            pltpu.VMEM(dealt, weight.dtype),
            pltpu.SemaphoreType.DMA((2, pieces)),
        ],
        compiler_params=pltpu.CompilerParams(vmem_limit_bytes=VMEM_LIMIT),
        cost_estimate=cost(COST_OWN),
        name="own",
    )(queries, keys, values, seens, starts, passages, rights, finals, weight)


ROWS = 512
LSE_ROWS = 32
ANY = pl.BlockSpec(memory_space=pl.ANY)
SCALARS = pl.BlockSpec(memory_space=pltpu.SMEM)
WHOLE = pl.BlockSpec(memory_space=pltpu.VMEM)


def meet(q, keys, values, state):
    rows = keys.shape[0]
    k = keys[...]
    v = values[...]
    s = contract_last(q, jnp.concatenate([k, k], axis=1))
    top = jnp.max(s, axis=1, keepdims=True)
    if state is None:
        new = jnp.broadcast_to(top, (q.shape[0], C))
    else:
        new = jnp.maximum(state[0], top)
    p = jnp.exp2(s - jnp.tile(new, (1, rows // C))).astype(BF16)
    pv = jnp.dot(p, jnp.concatenate([v, jnp.ones_like(v)], axis=1), preferred_element_type=F32)
    if state is None:
        return new, pv[:, C:], pv[:, :C]
    shrink = jnp.exp2(state[0] - new)
    return new, state[1] * shrink + pv[:, C:], state[2] * shrink + pv[:, :C]


def settle(out, mx, ls, acc):
    rows = mx.shape[0]
    row = lax.broadcasted_iota(jnp.int32, (C, C), 0)
    col = lax.broadcasted_iota(jnp.int32, (C, C), 1)
    out[pl.ds(0, rows), :] = (acc[...] / ls[...]).astype(BF16)
    lines = []
    for n in range(rows // C):
        here = pl.ds(n * C, C)
        lse = mx[here, :] + jnp.log2(ls[here, :])
        lines.append(jnp.sum(jnp.where(row == col, lse, 0.0), axis=0, keepdims=True))
    lse = jnp.concatenate(lines, axis=0)
    high = lse.astype(BF16).astype(F32)
    middle = (lse - high).astype(BF16).astype(F32)
    low = lse - high - middle
    out[pl.ds(rows, LSE_ROWS), :] = jnp.concatenate([high, middle, low, jnp.zeros_like(lse)], axis=0).astype(BF16)


def row_kernel(place, moved, t1, t2, s1, k2, v2, s3, out, mx, ls, acc, mv):
    y = place[1]
    rows = moved.shape[0]
    parts = [(s.at[pl.ds(0, rows)], s.at[pl.ds(rows, rows)]) for s in (s1, s3)]
    parts.insert(1, (k2, v2))
    for count in range(1, SIDE):

        @pl.when(y == count)
        def _(count=count):
            for d, (t, shard) in enumerate(zip((t1, t2, None)[:count], parts)):
                for b in range(rows // ROWS):
                    here = pl.ds(b * ROWS, ROWS)
                    q = mv[here, :] if d else moved[here, :]
                    state = (mx[here, :], ls[here, :], acc[here, :]) if d else None
                    mx[here, :], ls[here, :], acc[here, :] = meet(q, *shard, state)
                    if d + 1 < count:
                        mv[here, :] = left(nn(q, stacked(t[...])))
            settle(out, mx, ls, acc)


def row(place, moved, steps, shards):
    rows = moved.shape[0]
    return pl.pallas_call(
        row_kernel,
        out_shape=jax.ShapeDtypeStruct((rows + LSE_ROWS, C), BF16),
        in_specs=[SCALARS] + [WHOLE] * 7,
        out_specs=WHOLE,
        scratch_shapes=[pltpu.VMEM((rows, C), F32)] * 3 + [pltpu.VMEM((rows, 2 * C), BF16)],
        compiler_params=pltpu.CompilerParams(vmem_limit_bytes=VMEM_LIMIT),
        cost_estimate=cost(COST_ROW),
        name="row",
    )(place, moved, steps[1], steps[2], *shards[1:])


def visit(out, query, moves, shards, mx, ls, acc):
    rows = mx.shape[0]
    for d in range(SIDE):
        for b in range(rows // ROWS):
            here = pl.ds(b * ROWS, ROWS)
            q = left(nn(query[here, :], stacked(moves[d])))
            state = None if d == 0 else (mx[here, :], ls[here, :], acc[here, :])
            mx[here, :], ls[here, :], acc[here, :] = meet(q, *shards[d], state)
    settle(out, mx, ls, acc)


def parted(s0, s1, k2, v2, s3):
    rows = k2.shape[0]
    return [(s0.at[pl.ds(0, rows)], s0.at[pl.ds(rows, rows)]), (s1.at[pl.ds(0, rows)], s1.at[pl.ds(rows, rows)])] + [
        (k2, v2),
        (s3.at[pl.ds(0, rows)], s3.at[pl.ds(rows, rows)]),
    ]


def pair_kernel(place, suffixes, s0, s1, k2, v2, s3, q1, q3, link1, link2, out1, out3, moves2, mx, ls, acc, moves3):
    shards = parted(s0, s1, k2, v2, s3)

    @pl.when(place[0] + 1 < SIDE)
    def _():
        one = link1[...]
        both = left(nn(link2[...], stacked(one)))
        for d in range(SIDE):
            move = stacked(suffixes[d])
            moves2[d] = left(nn(one, move))
            moves3[d] = left(nn(both, move))
        visit(out1, q1, suffixes, shards, mx, ls, acc)

    @pl.when(place[0] + 3 < SIDE)
    def _():
        visit(out3, q3, moves3, shards, mx, ls, acc)


def last_kernel(place, moves, s0, s1, k2, v2, s3, q2, out, mx, ls, acc):
    @pl.when(place[0] + 2 < SIDE)
    def _():
        visit(out, q2, moves, parted(s0, s1, k2, v2, s3), mx, ls, acc)


def visitors(place, suffixes, shards, queries, links):
    rows = queries[0].shape[0] - C
    back = jax.ShapeDtypeStruct((rows + LSE_ROWS, C), BF16)
    moves = (SIDE, C, 2 * C)
    specs = [pl.BlockSpec((rows, 2 * C), lambda i: (0, 0))] * len(queries)
    specs += [pl.BlockSpec((C, 2 * C), lambda i, n=link.shape[0] // C - 1: (n, 0)) for link in links]
    return pl.pallas_call(
        pair_kernel if links else last_kernel,
        out_shape=(back, back, jax.ShapeDtypeStruct(moves, BF16)) if links else back,
        grid=(1,),
        in_specs=[SCALARS] + [WHOLE] * (2 + SIDE) + specs,
        out_specs=(WHOLE,) * 3 if links else WHOLE,
        scratch_shapes=[pltpu.VMEM((rows, C), F32)] * 3 + ([pltpu.VMEM(moves, BF16)] if links else []),
        compiler_params=pltpu.CompilerParams(vmem_limit_bytes=VMEM_LIMIT),
        cost_estimate=cost(COST_PAIR if links else COST_VISIT),
        name="pair" if links else "last",
    )(place, suffixes, *shards, *queries, *links)


def merge_kernel(place, inside, own_row, r1, r2, r3, whole, *parts):
    rows = whole.shape[0]
    blocks = rows // C
    partials = ((inside, None), (own_row, place[1] > 0), (r1, place[0] > 0), (r2, place[0] > 1), (r3, place[0] > 2))
    lines = []
    for r, there in partials:
        tail = r[pl.ds(rows, LSE_ROWS), :].astype(F32)
        lse = tail[0:blocks] + tail[blocks : 2 * blocks] + tail[2 * blocks : 3 * blocks]
        lines.append(lse if there is None else jnp.where(there, lse, NEGATIVE))
    top = lines[0]
    for line in lines[1:]:
        top = jnp.maximum(top, line)
    shares = [jnp.exp2(line - top) for line in lines]
    total = shares[0] + shares[1] + shares[2] + shares[3] + shares[4]
    shares = [share / total for share in shares]
    for n in range(blocks):
        here = pl.ds(n * C, C)
        summed = None
        for share, (r, there) in zip(shares, partials):
            one = jnp.transpose(jnp.broadcast_to(share[n : n + 1, :], (C, C))) * r[here, :].astype(F32)
            summed = one if there is None else summed + jnp.where(there, one, 0.0)
        done = summed.astype(BF16)
        whole[here, :] = done
        each = blocks // len(parts)
        parts[n // each][pl.ds(n % each * C, C), :] = done


def merge(place, partials):
    rows = partials[0].shape[0] - LSE_ROWS
    return pl.pallas_call(
        merge_kernel,
        out_shape=(jax.ShapeDtypeStruct((rows, C), BF16),) + (jax.ShapeDtypeStruct((rows // 2, C), BF16),) * 2,
        in_specs=[SCALARS] + [WHOLE] * 5,
        out_specs=(WHOLE,) * 3,
        compiler_params=pltpu.CompilerParams(vmem_limit_bytes=VMEM_LIMIT),
        cost_estimate=cost(2),
        name="merge",
    )(place, *partials)


def along_y(x, d):
    return lax.ppermute(x, "ctx", [(i, i - i % SIDE + (i + d) % SIDE) for i in range(SIDE * SIDE)])


def down_x(x, d):
    return lax.ppermute(x, "ctx", [(i, i - SIDE * d) for i in range(SIDE * d, SIDE * SIDE)])


def up_x(x, d):
    return lax.ppermute(x, "ctx", [(i, i + SIDE * d) for i in range(SIDE * SIDE - SIDE * d)])


def along_z(x, d):
    return lax.ppermute(x, "head", [(i, (i + 2 * d) % (2 * SIDE)) for i in range(2 * SIDE)])


def other_core(x):
    return lax.ppermute(x, "head", [(i, i ^ 1) for i in range(2 * SIDE)])


def body(queries, keys, values, house, rates, out_weight):
    rows = queries.shape[0]
    blocks = rows // C
    number = lax.axis_index("ctx")
    head = lax.axis_index("head")
    place = jnp.stack([number // SIDE, number % SIDE, head // 2, head % 2]).astype(jnp.int32)
    q, k, v, h = (x[:, 0, :] for x in (queries, keys, values, house))
    step, sent, passages, prefixes, applied, rights, finals, unit = transport(k, v, h, rates.reshape(blocks, C))
    steps = [step] + [along_y(step, d) for d in (1, 2, 3)]
    leaving, whole, suffixes, seens, starts = lead(place, q, prefixes, applied, unit, steps)
    first, third, second_link = down_x(leaving, 1), down_x(leaving, 3), down_x(whole, 2)
    before, after = along_y(sent, 1), along_y(sent, 3)
    moved, inside, dealt = own(q, k, v, seens, starts, passages, rights, finals, out_weight)
    before, after, dealt = lax.optimization_barrier((before, after, dealt))
    columns = lax.all_to_all(dealt, "head", split_axis=0, concat_axis=0, tiled=True)
    shards = [sent, before, along_y(before[:rows], 1), along_y(after[rows:], 3), after]
    relayed, moved = lax.optimization_barrier((first, moved))
    second = down_x(relayed, 1)
    one, three, moves = visitors(place, suffixes, shards, [first, third], [first, second_link])
    two = visitors(place, moves, shards, [second], [])
    returned = [up_x(one, 1), up_x(two, 2), up_x(three, 3)]
    own_row = row(place, moved, steps, shards)
    attended, top, low = merge(place, [inside, own_row, *returned])
    left_top, right_low = along_z(top, 1), along_z(low, 3)
    left_low, right_top = along_z(low, 1), along_z(top, 3)
    upper, lower = along_z(left_top, 1), along_z(right_low, 3)
    pieces = [attended, left_top, left_low, right_top, right_low, upper, lower]
    chips = jnp.concatenate(pieces, axis=0).reshape(SIDE, rows, C)

    def weights(core, offsets):
        return jnp.stack(
            [lax.dynamic_index_in_dim(columns, 2 * ((place[2] + d) % SIDE) + core, 0, False) for d in offsets]
        )

    def part(x, core, offsets):
        return jnp.einsum("srk,skn->rn", x, weights(core, offsets), preferred_element_type=F32)

    mine, theirs = place[3], 1 - place[3]
    offsets = (0, SIDE - 1, 1, 2)
    there, projected = lax.optimization_barrier((other_core(chips), part(chips, mine, offsets)))
    projected = projected + part(there, theirs, offsets)
    return (attended[:, None, :], projected.astype(BF16))


def solution(mesh):
    in_specs = (
        P("ctx", "head", None),
        P("ctx", "head", None),
        P("ctx", "head", None),
        P("ctx", "head", None),
        P("head", "ctx"),
        P("head", None),
    )
    out_specs = (P("ctx", "head", None), P("ctx", "head"))
    return jax.shard_map(body, mesh=mesh, in_specs=in_specs, out_specs=out_specs, check_vma=False)
```
